32 devices in a mesh: lon: 8 (over y, x, core), lat: 4 (over z).
Axes of the slice: x: 2, y: 2, z: 4, core: 2. Of those that a mesh axis runs over, the one named last changes fastest.
Arguments:
- adj_tracer: float32 [2, 8, 256, 1024], P(None, None, 'lat', 'lon'), may hold values from -108 to 108
- zonal_flow: bfloat16 [2, 8, 256, 1024], P(None, None, 'lat', 'lon'), may hold values from -0.25 to 0.25
- meridional_flow: bfloat16 [2, 8, 256, 1024], P(None, None, 'lat', 'lon'), may hold values from -0.25 to 0.25
- depth: int32 [256, 1024], P('lat', 'lon'), may hold values from 0 to 8
- coupling: float32 [2, 8], replicated, may hold values from -1 to 1
- surface_diag: float32 [256, 1024], P('lat', 'lon'), may hold values from 0.02 to 0.5
Outputs:
- tracer_adjoint: float32 [2, 8, 256, 1024], P(None, None, 'lat', 'lon')
- surface_sens: float32 [256, 1024], P('lat', 'lon')
The draws below stay inside these ranges and needn't reach their ends.
All inputs are finite; a program needn't handle non-finite values.
Results may differ from the reference program's by a relative error of at most 0.0003.
Values sent between devices are 32-bit elements; how exact they have to be, the bound alone decides.
No kernel may reach another device: no remote copies, remote signals or barrier semaphores. Data moves between devices by JAX's collectives and lax.ppermute only.
A program may use at most 64 MiB of HBM per device.

```python
import math
import jax
import jax.numpy as jnp

TRACERS = 2
K = 8
STEPS = 2
ITERS = 2
NX = 1024
NY = 256


def draw_adj_tracer(key, part):
    normal_key, row_key, col_key = jax.random.split(key, 3)
    array_shape = (TRACERS, K, NY, NX)
    row_frac = jnp.arange(NY, dtype=jnp.float32) / max(NY - 1, 1)
    col_frac = jnp.arange(NX, dtype=jnp.float32) / max(NX - 1, 1)
    row_scale = 3.0 ** row_frac * 10.0 ** (0.5 * jax.random.uniform(row_key, (NY,), jnp.float32))
    col_scale = 3.0 ** col_frac * 10.0 ** (0.5 * jax.random.uniform(col_key, (NX,), jnp.float32))
    base_draw = jnp.clip(jax.random.normal(normal_key, array_shape, jnp.float32), -4.0, 4.0)
    return (0.3 * base_draw * row_scale[:, None] * col_scale[None, :]).astype(jnp.float32)


def with_ends(array, rng, low, largest):
    longest = array.shape.index(max(array.shape))
    spots = []
    for shift in (0, 1):
        where = [jax.random.randint(jax.random.fold_in(rng, axis), (), 0, length) for axis, length in enumerate(array.shape)]
        where[longest] = (where[longest] + shift) % array.shape[longest]
        spots.append(tuple(where))
    return array.at[spots[0]].set(low).at[spots[1]].set(largest)


def level_of(key, dims, cuts, least, high):
    factor_of = 1.0
    for axis_at, blocks in cuts:
        heights = jax.random.uniform(jax.random.fold_in(jax.random.fold_in(key, 6), axis_at), (blocks,), jnp.float32, least / len(cuts), high / len(cuts))
        factor_of = factor_of * jnp.repeat(jnp.exp(heights), dims[axis_at] // blocks).reshape((-1,) + (1,) * (len(dims) - 1 - axis_at))
    return factor_of


def setup_inputs(seed: int = 0) -> dict:
    keys = jax.random.split(jax.random.key(seed), 7)
    return {
        "adj_tracer": draw_adj_tracer(jax.random.fold_in(keys[6], 71), 0),
        "zonal_flow": jnp.clip(jax.random.uniform(keys[1], (STEPS, K, NY, NX), jnp.float32, -0.25, 0.25) * level_of(keys[1], (STEPS, K, NY, NX), ((2, 4), (3, 8)), -0.4, 0.0), -0.25, 0.25).astype(jnp.bfloat16),
        "meridional_flow": jnp.clip(jax.random.uniform(keys[2], (STEPS, K, NY, NX), jnp.float32, -0.25, 0.25) * level_of(keys[2], (STEPS, K, NY, NX), ((2, 4), (3, 8)), -0.4, 0.0), -0.25, 0.25).astype(jnp.bfloat16),
        "depth": with_ends(jax.random.randint(keys[3], (NY, NX), 0, K + 1), jax.random.fold_in(keys[3], 1), 0, K).astype(jnp.int32),
        "coupling": jnp.clip(jax.random.uniform(keys[4], (TRACERS, K), jnp.float32, -1.0, 1.0), -1.0, 1.0),
        "surface_diag": jnp.clip(jnp.exp(math.log(0.5) - 3.218876 * jax.random.uniform(keys[5], (NY, NX), jnp.float32) ** level_of(keys[5], (NY, NX), ((0, 4), (1, 8)), -0.2, 0.2)), 0.02, 0.5),
    }


diffusion = 0.15


def west_of(source):
    return jnp.roll(source, 1, axis=-1)


def east_of(source):
    return jnp.roll(source, -1, axis=-1)


def south_of(source):
    border = jnp.zeros_like(source[..., :1, :])
    return jnp.concatenate([border, source[..., :-1, :]], axis=-2)


def north_of(source):
    border = jnp.zeros_like(source[..., :1, :])
    return jnp.concatenate([source[..., 1:, :], border], axis=-2)


def helmholtz(surface, surface_diag):
    beside = west_of(surface) + east_of(surface) + south_of(surface) + north_of(surface)
    return (surface_diag + 4.0) * surface - beside


def surface_solve(surface_rhs, surface_diag):
    surface_sol = jnp.zeros_like(surface_rhs)
    residual = surface_rhs
    direction = surface_rhs
    norm_now = jnp.sum(residual * residual)
    for iteration in range(ITERS):
        image_field = helmholtz(direction, surface_diag)
        step_length = norm_now / jnp.sum(direction * image_field)
        surface_sol = surface_sol + step_length * direction
        residual = residual - step_length * image_field
        norm_next = jnp.sum(residual * residual)
        direction = residual + (norm_next / norm_now) * direction
        norm_now = norm_next
    return surface_sol


def transpose_advect(middle, wet_cells, zonal_half, meridional_half, wet_west, wet_east, wet_south, wet_north):
    flux_sum = wet_west * (zonal_half - diffusion) * (west_of(middle) - middle)
    flux_sum = flux_sum + wet_east * (zonal_half + diffusion) * (middle - east_of(middle))
    flux_sum = flux_sum + wet_south * (meridional_half - diffusion) * (south_of(middle) - middle)
    flux_sum = flux_sum + wet_north * (meridional_half + diffusion) * (middle - north_of(middle))
    return middle - wet_cells * flux_sum


def reference(adj_tracer, zonal_flow, meridional_flow, depth, coupling, surface_diag):
    levels = jnp.arange(K, dtype=jnp.int32).reshape(K, 1, 1)
    wet_cells = (levels < depth[None]).astype(jnp.float32)
    wet_west = (levels < west_of(depth)[None]).astype(jnp.float32)
    wet_east = (levels < east_of(depth)[None]).astype(jnp.float32)
    wet_south = (levels < south_of(depth)[None]).astype(jnp.float32)
    wet_north = (levels < north_of(depth)[None]).astype(jnp.float32)
    weights = coupling[:, :, None, None]
    adjoint = adj_tracer
    surface_sens = jnp.zeros(surface_diag.shape, jnp.float32)
    for instant in reversed(range(STEPS)):
        masked = wet_cells[None] * adjoint
        surface_rhs = jnp.sum(weights * masked, axis=(0, 1))
        surface_sol = surface_solve(surface_rhs, surface_diag)
        surface_sens = surface_sens + surface_sol
        middle = masked + wet_cells[None] * weights * surface_sol[None, None]
        zonal_half = 0.5 * zonal_flow[instant].astype(jnp.float32)
        meridional_half = 0.5 * meridional_flow[instant].astype(jnp.float32)
        updated = []
        for tracer_index in range(TRACERS):
            updated.append(transpose_advect(middle[tracer_index], wet_cells, zonal_half, meridional_half, wet_west, wet_east, wet_south, wet_north))
        adjoint = jnp.stack(updated, axis=0)
    return adjoint, surface_sens
```

```python
import jax
import jax.numpy as jnp
from jax import lax
from jax.experimental import pallas as pl
from jax.experimental.pallas import tpu as pltpu
from jax.sharding import PartitionSpec as P

DIFF = 0.15
SHIFT = 4.0
LANES = 128
ROWS = 64
HALO = 8
EXT = ROWS + 2 * HALO
PAD = EXT + 2 * HALO
CHUNKS = EXT // 8
FLOW_AT, MASK_AT, DEPTH_AT, DIAG_AT, MSG_ROWS = 8, 40, 104, 108, 120
DEP, DIA, B, H, U, V, W, HU, HV, HW = range(10)
PAIRS = ((0, 0), (0, 1), (0, 2), (1, 1), (1, 2), (2, 2))
NSUMS = 4 + 4 * len(PAIRS)


def lane_iota():
    return lax.broadcasted_iota(jnp.int32, (8, LANES), 1)


def roll(x, by):
    by = by % LANES
    return pltpu.roll(x, by, 1) if by else x


def over_groups(x):
    for by in (8, 16, 32, 64):
        x = x + roll(x, by)
    return x


def in_every_group(x, group):
    lane = lane_iota()
    return over_groups(jnp.where(lane // 8 == group, x, 0.0))


def level_rows(ref, at, count, index, south):
    start = at + count * index
    return ref[pl.ds(start - (8 - count) if south else start, 8), :]


def row_messages(coupling_free_refs):
    adj_ref, zon_ref, mer_ref, depth_ref, diag_ref, a_ref, b_ref = coupling_free_refs
    even = lax.rem(lax.axis_index("lat"), 2) == 0
    zero = jnp.zeros((8, LANES), jnp.float32)
    for ref in (a_ref, b_ref):
        ref[0:8, :] = zero
        ref[MSG_ROWS - 8 : MSG_ROWS, :] = zero

    def put(at, low, high):
        count = low.shape[0]
        a_ref[pl.ds(at, count), :] = jnp.where(even, high, low)
        b_ref[pl.ds(at, count), :] = jnp.where(even, low, high)

    depth_low = depth_ref[0:4, :].astype(jnp.float32)
    depth_high = depth_ref[ROWS - 4 : ROWS, :].astype(jnp.float32)
    for level in range(16):
        k = float(level % 8)
        low = jnp.where(depth_low > k, adj_ref[level, 0:4, :], 0.0)
        high = jnp.where(depth_high > k, adj_ref[level, ROWS - 4 : ROWS, :], 0.0)
        put(MASK_AT + 4 * level, low, high)
    put(DEPTH_AT, depth_low, depth_high)
    put(DIAG_AT, diag_ref[0:4, :], diag_ref[ROWS - 4 : ROWS, :])
    for which, ref in enumerate((zon_ref, mer_ref)):
        for k in range(8):
            low = 0.5 * ref[0, k, 0:16, :].astype(jnp.float32)
            high = 0.5 * ref[0, k, ROWS - 16 : ROWS, :].astype(jnp.float32)
            put(FLOW_AT + 2 * (8 * which + k), low[0:2], high[14:16])


def row_message_kernel(*refs):
    row_messages(refs)


def sort_rows(recv_a_ref, recv_b_ref, south_ref, north_ref, last):
    lat = lax.axis_index("lat")
    even = lax.rem(lat, 2) == 0
    for start in range(0, MSG_ROWS, 8):
        a = recv_a_ref[pl.ds(start, 8), :]
        b = recv_b_ref[pl.ds(start, 8), :]
        south_ref[pl.ds(start, 8), :] = jnp.where(lat == 0, 0.0, jnp.where(even, b, a))
        north_ref[pl.ds(start, 8), :] = jnp.where(lat == last, 0.0, jnp.where(even, a, b))


def make_pack_kernel(last):
    def kernel(adj_ref, zon_ref, mer_ref, depth_ref, diag_ref, ra_ref, rb_ref, o_ref, south_ref, north_ref):
        sort_rows(ra_ref, rb_ref, south_ref, north_ref, last)

        def group_of(shape):
            return lax.broadcasted_iota(jnp.int32, shape, 1) // 8

        group = group_of((ROWS, LANES))
        depth = depth_ref[...].astype(jnp.float32)
        packed = jnp.zeros((ROWS, LANES), jnp.float32)
        for level in range(16):
            value = jnp.where(depth > float(level % 8), adj_ref[level], 0.0)
            packed = jnp.where(group == level, roll(value, 8 * level + 4), packed)
        o_ref[HALO : HALO + ROWS, :] = packed
        for which, ref in enumerate((zon_ref, mer_ref)):
            for k in range(8):
                level = 8 * which + k
                value = 0.5 * ref[0, k].astype(jnp.float32)
                packed = jnp.where(group == level, roll(value, 8 * level + 4), packed)
        o_ref[EXT + HALO : EXT + HALO + ROWS, :] = packed
        packed = jnp.where(group == 0, roll(depth, 4), roll(diag_ref[...], 12))
        o_ref[2 * EXT + HALO : 2 * EXT + HALO + ROWS, :] = packed
        group = group_of((8, LANES))
        for ref, south, base in ((south_ref, True, 0), (north_ref, False, HALO + ROWS)):
            packed = jnp.zeros((8, LANES), jnp.float32)
            for level in range(16):
                value = level_rows(ref, MASK_AT, 4, level, south)
                packed = jnp.where(group == level, roll(value, 8 * level + 4), packed)
            o_ref[base : base + 8, :] = packed
            for level in range(16):
                value = level_rows(ref, FLOW_AT, 2, level, south)
                packed = jnp.where(group == level, roll(value, 8 * level + 4), packed)
            o_ref[EXT + base : EXT + base + 8, :] = packed
            dep = level_rows(ref, DEPTH_AT, 4, 0, south)
            dia = level_rows(ref, DIAG_AT, 4, 0, south)
            packed = jnp.where(group == 0, roll(dep, 4), roll(dia, 12))
            o_ref[2 * EXT + base : 2 * EXT + base + 8, :] = packed

    return kernel


def make_fields_kernel(last, devices):
    def kernel(
        c_ref, adj_ref, zon_ref, mer_ref, depth_ref, diag_ref, ra_ref, rb_ref, o_ref, pa_ref, pb_ref,
        am_ref, pq_ref, f_out_ref, z_out_ref, sums_ref,
        south_ref, north_ref, m_ref, f_ref, s_ref, sm_ref, sf_ref,
    ):
        lane = lane_iota()
        pos = lane % 8
        group = lane // 8
        inner = pos < 4
        level_of = (group % 8).astype(jnp.float32)
        lat = lax.axis_index("lat")
        even_lon = lax.rem(lax.axis_index("lon"), 2) == 0
        coup = [c_ref[level // 8, level % 8] for level in range(16)]
        square = [coup[k] * coup[k] + coup[k + 8] * coup[k + 8] for k in range(8)]
        coup_lane = jnp.zeros((8, LANES), jnp.float32)
        for level in range(16):
            coup_lane = jnp.where(group == level, coup[level], coup_lane)
        square_lane = coup_lane * coup_lane

        sort_rows(ra_ref, rb_ref, south_ref, north_ref, last)
        depth = depth_ref[...].astype(jnp.float32)
        lo, hi = HALO, HALO + EXT - 8
        mid = 2 * HALO
        for level in range(16):
            m_ref[level, mid : mid + ROWS, :] = jnp.where(depth > float(level % 8), adj_ref[level], 0.0)
            m_ref[level, lo : lo + 8, :] = level_rows(south_ref, MASK_AT, 4, level, True)
            m_ref[level, hi : hi + 8, :] = level_rows(north_ref, MASK_AT, 4, level, False)
            flow = (zon_ref, mer_ref)[level // 8][0, level % 8]
            f_ref[level, mid : mid + ROWS, :] = 0.5 * flow.astype(jnp.float32)
            f_ref[level, lo : lo + 8, :] = level_rows(south_ref, FLOW_AT, 2, level, True)
            f_ref[level, hi : hi + 8, :] = level_rows(north_ref, FLOW_AT, 2, level, False)
        s_ref[DEP, 0, mid : mid + ROWS, :] = depth
        s_ref[DIA, 0, mid : mid + ROWS, :] = diag_ref[...]
        for field, at in ((DEP, DEPTH_AT), (DIA, DIAG_AT)):
            s_ref[field, 0, lo : lo + 8, :] = level_rows(south_ref, at, 4, 0, True)
            s_ref[field, 0, hi : hi + 8, :] = level_rows(north_ref, at, 4, 0, False)

        def sides(r, carry):
            at = pl.ds(pl.multiple_of(HALO + 8 * r, 8), 8)
            for part in range(3):
                src = pl.ds(pl.multiple_of(part * EXT + 8 * r, 8), 8)
                own = o_ref[src, :]
                pa = pa_ref[src, :]
                pb = pb_ref[src, :]
                east = jnp.where(inner, own, jnp.where(even_lon, pa, pb))
                west = jnp.where(inner, jnp.where(even_lon, pb, pa), own)
                for side, value in ((1, east), (2, west)):
                    if part == 0:
                        sm_ref[side - 1, at, :] = value
                        s_ref[B, side, at, :] = over_groups(coup_lane * value)
                    elif part == 1:
                        sf_ref[side - 1, at, :] = value
                    else:
                        s_ref[DEP, side, at, :] = in_every_group(value, 0)
                        s_ref[DIA, side, at, :] = in_every_group(value, 1)
            total = coup[0] * m_ref[0, at, :]
            for level in range(1, 16):
                total = total + coup[level] * m_ref[level, at, :]
            s_ref[B, 0, at, :] = total
            return carry

        lax.fori_loop(0, CHUNKS, sides, 0)

        def rows_at(r, shift=0):
            start = HALO + 8 * r
            return pl.ds(pl.multiple_of(start, 8) if shift == 0 else start + shift, 8)

        def wrap(main, west, east):
            return roll(jnp.where(inner, west, east), -4)

        def west_east(main, z):
            return roll(jnp.where(lane == LANES - 1, z, main), 1), roll(jnp.where(lane == 0, z, main), -1)

        def star(field, part, r):
            centre = s_ref[field, part, rows_at(r), :]
            south = s_ref[field, part, rows_at(r, -1), :]
            north = s_ref[field, part, rows_at(r, 1), :]
            if part == 0:
                z = wrap(centre, s_ref[field, 2, rows_at(r), :], s_ref[field, 1, rows_at(r), :])
                west, east = west_east(centre, z)
            else:
                west, east = roll(centre, 1), roll(centre, -1)
            return centre, west, east, south, north

        def shifted(field, part, r):
            centre, west, east, south, north = star(field, part, r)
            return s_ref[DIA, part, rows_at(r), :] * centre - (west + east + south + north)

        row = lax.broadcasted_iota(jnp.int32, (8, LANES), 0)

        def on_grid(r, value):
            at = 8 * r + row - HALO
            beyond = ((at < 0) & (lat == 0)) | ((at >= ROWS) & (lat == last))
            return jnp.where(beyond, 0.0, value)

        def images(r, carry):
            for part in range(3):
                s_ref[H, part, rows_at(r), :] = on_grid(r, shifted(B, part, r))
            return carry

        lax.fori_loop(0, CHUNKS, images, 0)

        def apply(coef, centre, west, east, south, north):
            c0, cw, ce, cs, cn = coef
            return c0 * centre + cw * west + ce * east + cs * south + cn * north

        def coefficients(u, w, mins, k):
            dep, dw, de, ds, dn = mins
            cw = jnp.where(dw > k, DIFF - u, 0.0)
            ce = jnp.where(de > k, DIFF + u, 0.0)
            cs = jnp.where(ds > k, DIFF - w, 0.0)
            cn = jnp.where(dn > k, DIFF + w, 0.0)
            c0 = jnp.where(dep > k, 1.0 - ((cw + ce) + (cs + cn)), 0.0)
            return c0, cw, ce, cs, cn

        def depths(part, r):
            dep, dw, de, ds, dn = star(DEP, part, r)
            return dep, jnp.minimum(dep, dw), jnp.minimum(dep, de), jnp.minimum(dep, ds), jnp.minimum(dep, dn)

        def advect(r, carry):
            out_at = pl.ds(pl.multiple_of(8 * r, 8), 8)
            at, below, above = rows_at(r), rows_at(r, -1), rows_at(r, 1)
            mins = depths(0, r)
            bs = star(B, 0, r)
            hs = star(H, 0, r)
            zm = jnp.where(inner, sm_ref[1, at, :], sm_ref[0, at, :])
            us = vs = ws = jnp.zeros((8, LANES), jnp.float32)
            for k in range(8):
                coef = coefficients(f_ref[k, at, :], f_ref[8 + k, at, :], mins, float(k))
                for level in (k, k + 8):
                    centre = m_ref[level, at, :]
                    west, east = west_east(centre, roll(zm, -(8 * level + 4)))
                    value = apply(coef, centre, west, east, m_ref[level, below, :], m_ref[level, above, :])
                    am_ref[level, out_at, :] = value
                    us = us + coup[level] * value
                p = apply(coef, *bs)
                q = apply(coef, *hs)
                pq_ref[k, out_at, :] = p
                pq_ref[8 + k, out_at, :] = q
                vs = vs + square[k] * p
                ws = ws + square[k] * q
            s_ref[U, 0, at, :] = us
            s_ref[V, 0, at, :] = vs
            s_ref[W, 0, at, :] = ws
            kept = []
            for part in (1, 2):
                mins = depths(part, r)
                flow = sf_ref[part - 1, at, :]
                turned = roll(flow, 64)
                u = jnp.where(lane < 64, flow, turned)
                w = jnp.where(lane < 64, turned, flow)
                coef = coefficients(u, w, mins, level_of)
                centre = sm_ref[part - 1, at, :]
                value = apply(
                    coef, centre, roll(centre, 1), roll(centre, -1),
                    sm_ref[part - 1, below, :], sm_ref[part - 1, above, :],
                )
                p = apply(coef, *star(B, part, r))
                q = apply(coef, *star(H, part, r))
                s_ref[U, part, at, :] = over_groups(coup_lane * value)
                s_ref[V, part, at, :] = over_groups(square_lane * p)
                s_ref[W, part, at, :] = over_groups(square_lane * q)
                kept.append((value, p, q))
            for slot in range(3):
                z_out_ref[slot, out_at, :] = jnp.where(inner, kept[1][slot], kept[0][slot])
            return carry

        lax.fori_loop(0, CHUNKS, advect, 0)

        def images_two(r, carry):
            for source, target in ((U, HU), (V, HV), (W, HW)):
                for part in range(3):
                    s_ref[target, part, rows_at(r), :] = on_grid(r, shifted(source, part, r))
            return carry

        lax.fori_loop(0, CHUNKS, images_two, 0)

        def gather(r, sums):
            at = rows_at(r)
            new = []
            b = s_ref[B, 0, at, :]
            h = s_ref[H, 0, at, :]
            new += [b * b, b * h, h * h, h * shifted(H, 0, r)]
            fields = [s_ref[field, 0, at, :] for field in (U, V, W)]
            image = [s_ref[field, 0, at, :] for field in (HU, HV, HW)]
            second = [shifted(field, 0, r) for field in (HU, HV, HW)]
            for left, right in ((fields, fields), (fields, image), (image, image), (image, second)):
                new += [left[i] * right[j] for i, j in PAIRS]
            return tuple(s + n for s, n in zip(sums, new))

        zero = jnp.zeros((8, LANES), jnp.float32)
        sums = lax.fori_loop(1, CHUNKS - 1, gather, (zero,) * NSUMS)
        line = jnp.zeros((1, LANES), jnp.float32)
        for index, value in enumerate(sums):
            total = jnp.sum(jnp.sum(value, axis=1, keepdims=True), axis=0, keepdims=True)
            line = jnp.where(lane[0:1, :] == index, total, line)
        sums_ref[...] = jnp.broadcast_to(line, (devices, LANES))

        def hand_over(r, carry):
            at = rows_at(r)
            out_at = pl.ds(pl.multiple_of(8 * r, 8), 8)
            for slot, field in enumerate((B, H, U, V, W, HU, HV, HW, DEP)):
                f_out_ref[slot, out_at, :] = s_ref[field, 0, at, :]
            for slot, field in enumerate((U, V, W, HU, HV, HW, DEP)):
                z_out_ref[3 + slot, out_at, :] = jnp.where(inner, s_ref[field, 2, at, :], s_ref[field, 1, at, :])
            return carry

        lax.fori_loop(0, CHUNKS, hand_over, 0)

    return kernel


def solve(m0, m1, m2, m3):
    mean = m1 / m0
    theta = mean + SHIFT
    spread = m2 - mean * m1
    ratio = spread / (theta * theta * m0)
    curve = m3 - 2.0 * mean * m2 + mean * mean * m1 + SHIFT * spread
    gamma = curve / spread - ratio * theta
    image_factor = -1.0 / (theta * gamma)
    return 1.0 / theta + (mean / theta + ratio) / gamma, image_factor


def finish_kernel(c_ref, zon_ref, mer_ref, am_ref, pq_ref, f_ref, z_ref, sums_ref, out_ref, sens_ref, m_ref, x_ref):
    lane = lane_iota()
    group = lane // 8
    level_of = (group % 8).astype(jnp.float32)
    coup = [c_ref[level // 8, level % 8] for level in range(16)]
    coup_lane = jnp.zeros((8, LANES), jnp.float32)
    for level in range(16):
        coup_lane = jnp.where(group == level, coup[level], coup_lane)

    line = jnp.sum(sums_ref[...], axis=0, keepdims=True)

    def total(index):
        return jnp.sum(jnp.where(lane[0:1, :] == index, line, 0.0), axis=1, keepdims=True)

    a1, e1 = solve(*[total(i) for i in range(4)])
    y = (None, a1, e1)
    factor = (None, a1 * 2.0, e1 * 2.0, a1 * a1, a1 * e1 * 2.0, e1 * e1)
    moments = []
    for kind in range(4):
        base = 4 + kind * len(PAIRS)
        value = total(base)
        for index in range(1, len(PAIRS)):
            value = value + factor[index] * total(base + index)
        moments.append(value)
    a0, e0 = solve(*moments)
    a1, e1, a0, e0 = [jnp.broadcast_to(v, (8, LANES)) for v in (a1, e1, a0, e0)]
    FB, FH, FU, FV, FW, FHU, FHV, FHW, FDEP = range(9)
    ZAM, ZP, ZQ, ZU, ZV, ZW, ZHU, ZHV, ZHW, ZDEP = range(10)

    def middle(r, carry):
        at = pl.ds(pl.multiple_of(8 * r, 8), 8)
        to = pl.ds(pl.multiple_of(8 * r + HALO, 8), 8)
        b = f_ref[FU, at, :] + a1 * f_ref[FV, at, :] + e1 * f_ref[FW, at, :]
        h = f_ref[FHU, at, :] + a1 * f_ref[FHV, at, :] + e1 * f_ref[FHW, at, :]
        x = a0 * b + e0 * h
        x_ref[at, :] = x + a1 * f_ref[FB, at, :] + e1 * f_ref[FH, at, :]
        dep = f_ref[FDEP, at, :]
        for k in range(8):
            both = a1 * pq_ref[k, at, :] + e1 * pq_ref[8 + k, at, :] + jnp.where(dep > float(k), x, 0.0)
            for level in (k, k + 8):
                m_ref[level, to, :] = am_ref[level, at, :] + coup[level] * both
        return carry

    lax.fori_loop(0, CHUNKS, middle, 0)
    sens_ref[...] = x_ref[HALO : HALO + ROWS, :]

    for k in range(16):
        m_ref[k, 0:8, :] = jnp.zeros((8, LANES), jnp.float32)

    def west_east(main, z):
        return roll(jnp.where(lane == LANES - 1, z, main), 1), roll(jnp.where(lane == 0, z, main), -1)

    def advect(r, carry):
        at = pl.ds(pl.multiple_of(8 * r + HALO, 8), 8)
        out_at = pl.ds(pl.multiple_of(8 * r, 8), 8)
        start = 8 * r + 2 * HALO
        here = pl.ds(pl.multiple_of(start, 8), 8)
        below, above = pl.ds(start - 1, 8), pl.ds(start + 1, 8)
        zb = z_ref[ZU, at, :] + a1 * z_ref[ZV, at, :] + e1 * z_ref[ZW, at, :]
        zh = z_ref[ZHU, at, :] + a1 * z_ref[ZHV, at, :] + e1 * z_ref[ZHW, at, :]
        zx = a0 * zb + e0 * zh
        zd = z_ref[ZDEP, at, :]
        zm = z_ref[ZAM, at, :] + coup_lane * (
            a1 * z_ref[ZP, at, :] + e1 * z_ref[ZQ, at, :] + jnp.where(zd > level_of, zx, 0.0)
        )
        dep = f_ref[FDEP, at, :]
        dw, de = west_east(dep, roll(zd, -4))
        ds = f_ref[FDEP, pl.ds(8 * r + HALO - 1, 8), :]
        dn = f_ref[FDEP, pl.ds(8 * r + HALO + 1, 8), :]
        dw, de, ds, dn = [jnp.minimum(dep, d) for d in (dw, de, ds, dn)]
        for k in range(8):
            u = 0.5 * zon_ref[0, k, out_at, :].astype(jnp.float32)
            w = 0.5 * mer_ref[0, k, out_at, :].astype(jnp.float32)
            cw = jnp.where(dw > float(k), DIFF - u, 0.0)
            ce = jnp.where(de > float(k), DIFF + u, 0.0)
            cs = jnp.where(ds > float(k), DIFF - w, 0.0)
            cn = jnp.where(dn > float(k), DIFF + w, 0.0)
            c0 = 1.0 - ((cw + ce) + (cs + cn))
            for level in (k, k + 8):
                centre = m_ref[level, here, :]
                west, east = west_east(centre, roll(zm, -(8 * level + 4)))
                out_ref[level, out_at, :] = (
                    c0 * centre + cw * west + ce * east + cs * m_ref[level, below, :] + cn * m_ref[level, above, :]
                )
        return carry

    lax.fori_loop(0, ROWS // 8, advect, 0)


def whole(shape):
    return pl.BlockSpec(shape, lambda i: (0,) * len(shape))


def step_flow(step):
    return pl.BlockSpec((1, 8, ROWS, LANES), lambda i: (step, 0, 0, 0))


def on_device_of(lon, lat):
    devices = lon * lat
    f32 = jnp.float32

    def array(*shape):
        return jax.ShapeDtypeStruct(shape, f32)

    smem = pl.BlockSpec(memory_space=pltpu.SMEM)
    params = pltpu.CompilerParams(vmem_limit_bytes=48 * 2**20)
    pairs = {}
    for axis, count in (("lon", lon), ("lat", lat)):
        first = [(i, i ^ 1) for i in range(count)]
        second = [(i, (i - 1) % count if i % 2 == 0 else (i + 1) % count) for i in range(count)]
        pairs[axis] = (first, second)

    def swap(axis, a, b):
        first, second = pairs[axis]
        return lax.ppermute(a, axis, first), lax.ppermute(b, axis, second)

    def on_device(adj_tracer, zonal_flow, meridional_flow, depth, coupling, surface_diag):
        adj = adj_tracer.reshape(16, ROWS, LANES)
        block = [whole((16, ROWS, LANES)), step_flow(1), step_flow(1), whole((ROWS, LANES)), whole((ROWS, LANES))]
        block_args = (adj, zonal_flow, meridional_flow, depth, surface_diag)
        message = whole((MSG_ROWS, LANES))
        msg_a, msg_b = pl.pallas_call(
            row_message_kernel,
            grid=(1,),
            in_specs=block,
            out_specs=[message, message],
            out_shape=[array(MSG_ROWS, LANES)] * 2,
            compiler_params=params,
            name="row_messages",
        )(*block_args)
        recv_a, recv_b = swap("lat", msg_a, msg_b)
        columns = whole((3 * EXT, LANES))
        row_scratch = [pltpu.VMEM((MSG_ROWS, LANES), f32)] * 2
        own = pl.pallas_call(
            make_pack_kernel(lat - 1),
            grid=(1,),
            in_specs=block + [message, message],
            out_specs=columns,
            out_shape=array(3 * EXT, LANES),
            scratch_shapes=row_scratch,
            compiler_params=params,
            name="pack_columns",
        )(*block_args, recv_a, recv_b)
        side_a, side_b = swap("lon", own, own)
        outs = [(16, EXT, LANES), (16, EXT, LANES), (9, EXT, LANES), (10, EXT, LANES), (devices, LANES)]
        am, pq, fields, zs, sums = pl.pallas_call(
            make_fields_kernel(lat - 1, devices),
            grid=(1,),
            in_specs=[smem] + block + [message, message, columns, columns, columns],
            out_specs=[whole(s) for s in outs],
            out_shape=[array(*s) for s in outs],
            scratch_shapes=row_scratch
            + [
                pltpu.VMEM((16, PAD, LANES), f32),
                pltpu.VMEM((16, PAD, LANES), f32),
                pltpu.VMEM((10, 3, PAD, LANES), f32),
                pltpu.VMEM((2, PAD, LANES), f32),
                pltpu.VMEM((2, PAD, LANES), f32),
            ],
            compiler_params=params,
            name="fields",
        )(coupling, *block_args, recv_a, recv_b, own, side_a, side_b)
        everyone = lax.all_to_all(sums, ("lon", "lat"), 0, 0, tiled=True)
        out, sens = pl.pallas_call(
            finish_kernel,
            grid=(1,),
            in_specs=[smem, step_flow(0), step_flow(0)] + [whole(s) for s in outs],
            out_specs=[whole((16, ROWS, LANES)), whole((ROWS, LANES))],
            out_shape=[array(16, ROWS, LANES), array(ROWS, LANES)],
            scratch_shapes=[pltpu.VMEM((16, PAD, LANES), f32), pltpu.VMEM((EXT, LANES), f32)],
            compiler_params=params,
            name="finish",
        )(coupling, zonal_flow, meridional_flow, am, pq, fields, zs, everyone)
        return out.reshape(adj_tracer.shape), sens

    return on_device


def solution(mesh):
    in_specs = (
        P(None, None, "lat", "lon"),
        P(None, None, "lat", "lon"),
        P(None, None, "lat", "lon"),
        P("lat", "lon"),
        P(),
        P("lat", "lon"),
    )
    out_specs = (P(None, None, "lat", "lon"), P("lat", "lon"))
    return jax.shard_map(
        on_device_of(mesh.shape["lon"], mesh.shape["lat"]),
        mesh=mesh, in_specs=in_specs, out_specs=out_specs, check_vma=False,
    )
```

```python
import jax
import jax.numpy as jnp
from jax import lax
from jax.experimental import pallas as pl
from jax.experimental.pallas import tpu as pltpu
from jax.sharding import PartitionSpec as P

DIFF = 0.15
SHIFT = 4.0
LANES = 128
ROWS = 64
HALO = 8
EXT = ROWS + 2 * HALO
PAD = EXT + 2 * HALO
CHUNKS = EXT // 8
FLOW_AT, MASK_AT, DEPTH_AT, DIAG_AT, MSG_ROWS = 8, 40, 104, 108, 120
DEP, DIA, B, H, U, V, W, HU, HV, HW = range(10)
PAIRS = ((0, 0), (0, 1), (0, 2), (1, 1), (1, 2), (2, 2))
NSUMS = 4 + 4 * len(PAIRS)


def lane_iota():
    return lax.broadcasted_iota(jnp.int32, (8, LANES), 1)


def roll(x, by):
    by = by % LANES
    return pltpu.roll(x, by, 1) if by else x


def over_groups(x):
    for by in (8, 16, 32, 64):
        x = x + roll(x, by)
    return x


def in_every_group(x, group):
    lane = lane_iota()
    return over_groups(jnp.where(lane // 8 == group, x, 0.0))


def level_rows(ref, at, count, index, south):
    start = at + count * index
    return ref[pl.ds(start - (8 - count) if south else start, 8), :]


def row_message_kernel(adj, zon, mer, depth, diag, a_ref, b_ref, adj_ref, flow_ref, depth_ref, diag_ref, sems):
    copies = []
    for edge, start in ((0, 0), (1, ROWS - 8)):
        rows = pl.ds(start, 8)
        for source, target in (
            (adj.at[:, rows, :], adj_ref.at[edge]),
            (zon.at[1, :, rows, :], flow_ref.at[edge, 0]),
            (mer.at[1, :, rows, :], flow_ref.at[edge, 1]),
            (depth.at[rows, :], depth_ref.at[edge]),
            (diag.at[rows, :], diag_ref.at[edge]),
        ):
            copies.append(pltpu.make_async_copy(source, target, sems.at[len(copies)]))
            copies[-1].start()
    even = lax.rem(lax.axis_index("lat"), 2) == 0
    zero = jnp.zeros((8, LANES), jnp.float32)
    for ref in (a_ref, b_ref):
        ref[0:8, :] = zero
        ref[MSG_ROWS - 8 : MSG_ROWS, :] = zero
    for copy in copies:
        copy.wait()

    def put(at, low, high):
        count = low.shape[0]
        a_ref[pl.ds(at, count), :] = jnp.where(even, high, low)
        b_ref[pl.ds(at, count), :] = jnp.where(even, low, high)

    depth_low = depth_ref[0, 0:4, :].astype(jnp.float32)
    depth_high = depth_ref[1, 4:8, :].astype(jnp.float32)
    for level in range(16):
        k = float(level % 8)
        low = jnp.where(depth_low > k, adj_ref[0, level, 0:4, :], 0.0)
        high = jnp.where(depth_high > k, adj_ref[1, level, 4:8, :], 0.0)
        put(MASK_AT + 4 * level, low, high)
    put(DEPTH_AT, depth_low, depth_high)
    put(DIAG_AT, diag_ref[0, 0:4, :], diag_ref[1, 4:8, :])
    for level in range(16):
        low = 0.5 * flow_ref[0, level // 8, level % 8].astype(jnp.float32)
        high = 0.5 * flow_ref[1, level // 8, level % 8].astype(jnp.float32)
        put(FLOW_AT + 2 * level, low[0:2], high[6:8])


def sort_rows(recv_a_ref, recv_b_ref, south_ref, north_ref, last):
    lat = lax.axis_index("lat")
    even = lax.rem(lat, 2) == 0
    for start in range(0, MSG_ROWS, 8):
        a = recv_a_ref[pl.ds(start, 8), :]
        b = recv_b_ref[pl.ds(start, 8), :]
        south_ref[pl.ds(start, 8), :] = jnp.where(lat == 0, 0.0, jnp.where(even, b, a))
        north_ref[pl.ds(start, 8), :] = jnp.where(lat == last, 0.0, jnp.where(even, a, b))


def make_pack_kernel(last):
    def kernel(adj_ref, zon_ref, mer_ref, depth_ref, diag_ref, ra_ref, rb_ref, o_ref, south_ref, north_ref):
        sort_rows(ra_ref, rb_ref, south_ref, north_ref, last)

        def group_of(shape):
            return lax.broadcasted_iota(jnp.int32, shape, 1) // 8

        group = group_of((ROWS, LANES))
        depth = depth_ref[...].astype(jnp.float32)
        packed = jnp.zeros((ROWS, LANES), jnp.float32)
        for level in range(16):
            value = jnp.where(depth > float(level % 8), adj_ref[level], 0.0)
            packed = jnp.where(group == level, roll(value, 8 * level + 4), packed)
        o_ref[HALO : HALO + ROWS, :] = packed
        for which, ref in enumerate((zon_ref, mer_ref)):
            for k in range(8):
                level = 8 * which + k
                value = 0.5 * ref[1, k].astype(jnp.float32)
                packed = jnp.where(group == level, roll(value, 8 * level + 4), packed)
        o_ref[EXT + HALO : EXT + HALO + ROWS, :] = packed
        packed = jnp.where(group == 0, roll(depth, 4), roll(diag_ref[...], 12))
        o_ref[2 * EXT + HALO : 2 * EXT + HALO + ROWS, :] = packed
        group = group_of((8, LANES))
        for ref, south, base in ((south_ref, True, 0), (north_ref, False, HALO + ROWS)):
            packed = jnp.zeros((8, LANES), jnp.float32)
            for level in range(16):
                value = level_rows(ref, MASK_AT, 4, level, south)
                packed = jnp.where(group == level, roll(value, 8 * level + 4), packed)
            o_ref[base : base + 8, :] = packed
            for level in range(16):
                value = level_rows(ref, FLOW_AT, 2, level, south)
                packed = jnp.where(group == level, roll(value, 8 * level + 4), packed)
            o_ref[EXT + base : EXT + base + 8, :] = packed
            dep = level_rows(ref, DEPTH_AT, 4, 0, south)
            dia = level_rows(ref, DIAG_AT, 4, 0, south)
            packed = jnp.where(group == 0, roll(dep, 4), roll(dia, 12))
            o_ref[2 * EXT + base : 2 * EXT + base + 8, :] = packed

    return kernel


def make_fields_kernel(last, devices):
    def kernel(
        c_ref, adj_ref, zon_ref, mer_ref, depth_ref, diag_ref, ra_ref, rb_ref, o_ref, pa_ref, pb_ref,
        am_ref, pq_ref, f_out_ref, z_out_ref, sums_ref,
        south_ref, north_ref, m_ref, f_ref, s_ref, sm_ref, sf_ref,
    ):
        lane = lane_iota()
        pos = lane % 8
        group = lane // 8
        inner = pos < 4
        level_of = (group % 8).astype(jnp.float32)
        lat = lax.axis_index("lat")
        even_lon = lax.rem(lax.axis_index("lon"), 2) == 0
        coup = [c_ref[level // 8, level % 8] for level in range(16)]
        square = [coup[k] * coup[k] + coup[k + 8] * coup[k + 8] for k in range(8)]
        coup_lane = jnp.zeros((8, LANES), jnp.float32)
        for level in range(16):
            coup_lane = jnp.where(group == level, coup[level], coup_lane)
        square_lane = coup_lane * coup_lane

        sort_rows(ra_ref, rb_ref, south_ref, north_ref, last)
        depth = depth_ref[...].astype(jnp.float32)
        lo, hi = HALO, HALO + EXT - 8
        mid = 2 * HALO
        for level in range(16):
            m_ref[level, mid : mid + ROWS, :] = jnp.where(depth > float(level % 8), adj_ref[level], 0.0)
            m_ref[level, lo : lo + 8, :] = level_rows(south_ref, MASK_AT, 4, level, True)
            m_ref[level, hi : hi + 8, :] = level_rows(north_ref, MASK_AT, 4, level, False)
            flow = (zon_ref, mer_ref)[level // 8][1, level % 8]
            f_ref[level, mid : mid + ROWS, :] = 0.5 * flow.astype(jnp.float32)
            f_ref[level, lo : lo + 8, :] = level_rows(south_ref, FLOW_AT, 2, level, True)
            f_ref[level, hi : hi + 8, :] = level_rows(north_ref, FLOW_AT, 2, level, False)
        s_ref[DEP, 0, mid : mid + ROWS, :] = depth
        s_ref[DIA, 0, mid : mid + ROWS, :] = diag_ref[...]
        for field, at in ((DEP, DEPTH_AT), (DIA, DIAG_AT)):
            s_ref[field, 0, lo : lo + 8, :] = level_rows(south_ref, at, 4, 0, True)
            s_ref[field, 0, hi : hi + 8, :] = level_rows(north_ref, at, 4, 0, False)

        def sides(r, carry):
            at = pl.ds(pl.multiple_of(HALO + 8 * r, 8), 8)
            for part in range(3):
                src = pl.ds(pl.multiple_of(part * EXT + 8 * r, 8), 8)
                own = o_ref[src, :]
                pa = pa_ref[src, :]
                pb = pb_ref[src, :]
                east = jnp.where(inner, own, jnp.where(even_lon, pa, pb))
                west = jnp.where(inner, jnp.where(even_lon, pb, pa), own)
                for side, value in ((1, east), (2, west)):
                    if part == 0:
                        sm_ref[side - 1, at, :] = value
                        s_ref[B, side, at, :] = over_groups(coup_lane * value)
                    elif part == 1:
                        sf_ref[side - 1, at, :] = value
                    else:
                        s_ref[DEP, side, at, :] = in_every_group(value, 0)
                        s_ref[DIA, side, at, :] = in_every_group(value, 1)
            total = coup[0] * m_ref[0, at, :]
            for level in range(1, 16):
                total = total + coup[level] * m_ref[level, at, :]
            s_ref[B, 0, at, :] = total
            return carry

        lax.fori_loop(0, CHUNKS, sides, 0, unroll=True)

        def rows_at(r, shift=0):
            start = HALO + 8 * r
            return pl.ds(pl.multiple_of(start, 8) if shift == 0 else start + shift, 8)

        def wrap(main, west, east):
            return roll(jnp.where(inner, west, east), -4)

        def west_east(main, z):
            return roll(jnp.where(lane == LANES - 1, z, main), 1), roll(jnp.where(lane == 0, z, main), -1)

        def star(field, part, r):
            centre = s_ref[field, part, rows_at(r), :]
            south = s_ref[field, part, rows_at(r, -1), :]
            north = s_ref[field, part, rows_at(r, 1), :]
            if part == 0:
                z = wrap(centre, s_ref[field, 2, rows_at(r), :], s_ref[field, 1, rows_at(r), :])
                west, east = west_east(centre, z)
            else:
                west, east = roll(centre, 1), roll(centre, -1)
            return centre, west, east, south, north

        def shifted(field, part, r):
            centre, west, east, south, north = star(field, part, r)
            return s_ref[DIA, part, rows_at(r), :] * centre - (west + east + south + north)

        row = lax.broadcasted_iota(jnp.int32, (8, LANES), 0)

        def on_grid(r, value):
            at = 8 * r + row - HALO
            beyond = ((at < 0) & (lat == 0)) | ((at >= ROWS) & (lat == last))
            return jnp.where(beyond, 0.0, value)

        def images(r, carry):
            for part in range(3):
                s_ref[H, part, rows_at(r), :] = on_grid(r, shifted(B, part, r))
            return carry

        lax.fori_loop(0, CHUNKS, images, 0, unroll=True)

        def apply(coef, centre, west, east, south, north):
            c0, cw, ce, cs, cn = coef
            return c0 * centre + cw * west + ce * east + cs * south + cn * north

        def coefficients(u, w, mins, k):
            dep, dw, de, ds, dn = mins
            cw = jnp.where(dw > k, DIFF - u, 0.0)
            ce = jnp.where(de > k, DIFF + u, 0.0)
            cs = jnp.where(ds > k, DIFF - w, 0.0)
            cn = jnp.where(dn > k, DIFF + w, 0.0)
            c0 = jnp.where(dep > k, 1.0 - ((cw + ce) + (cs + cn)), 0.0)
            return c0, cw, ce, cs, cn

        def depths(part, r):
            dep, dw, de, ds, dn = star(DEP, part, r)
            return dep, jnp.minimum(dep, dw), jnp.minimum(dep, de), jnp.minimum(dep, ds), jnp.minimum(dep, dn)

        def advect(r, carry):
            out_at = pl.ds(pl.multiple_of(8 * r, 8), 8)
            at, below, above = rows_at(r), rows_at(r, -1), rows_at(r, 1)
            mins = depths(0, r)
            bs = star(B, 0, r)
            hs = star(H, 0, r)
            zm = jnp.where(inner, sm_ref[1, at, :], sm_ref[0, at, :])
            us = vs = ws = jnp.zeros((8, LANES), jnp.float32)
            for k in range(8):
                coef = coefficients(f_ref[k, at, :], f_ref[8 + k, at, :], mins, float(k))
                for level in (k, k + 8):
                    centre = m_ref[level, at, :]
                    west, east = west_east(centre, roll(zm, -(8 * level + 4)))
                    value = apply(coef, centre, west, east, m_ref[level, below, :], m_ref[level, above, :])
                    am_ref[level, out_at, :] = value
                    us = us + coup[level] * value
                p = apply(coef, *bs)
                q = apply(coef, *hs)
                pq_ref[k, out_at, :] = p
                pq_ref[8 + k, out_at, :] = q
                vs = vs + square[k] * p
                ws = ws + square[k] * q
            s_ref[U, 0, at, :] = us
            s_ref[V, 0, at, :] = vs
            s_ref[W, 0, at, :] = ws
            kept = []
            for part in (1, 2):
                mins = depths(part, r)
                flow = sf_ref[part - 1, at, :]
                turned = roll(flow, 64)
                u = jnp.where(lane < 64, flow, turned)
                w = jnp.where(lane < 64, turned, flow)
                coef = coefficients(u, w, mins, level_of)
                centre = sm_ref[part - 1, at, :]
                value = apply(
                    coef, centre, roll(centre, 1), roll(centre, -1),
                    sm_ref[part - 1, below, :], sm_ref[part - 1, above, :],
                )
                p = apply(coef, *star(B, part, r))
                q = apply(coef, *star(H, part, r))
                s_ref[U, part, at, :] = over_groups(coup_lane * value)
                s_ref[V, part, at, :] = over_groups(square_lane * p)
                s_ref[W, part, at, :] = over_groups(square_lane * q)
                kept.append((value, p, q))
            for slot in range(3):
                z_out_ref[slot, out_at, :] = jnp.where(inner, kept[1][slot], kept[0][slot])
            return carry

        lax.fori_loop(0, CHUNKS, advect, 0)

        def images_two(r, carry):
            for source, target in ((U, HU), (V, HV), (W, HW)):
                for part in range(3):
                    s_ref[target, part, rows_at(r), :] = on_grid(r, shifted(source, part, r))
            return carry

        lax.fori_loop(0, CHUNKS, images_two, 0, unroll=True)

        def gather(r, sums):
            at = rows_at(r)
            new = []
            b = s_ref[B, 0, at, :]
            h = s_ref[H, 0, at, :]
            new += [b * b, b * h, h * h, h * shifted(H, 0, r)]
            fields = [s_ref[field, 0, at, :] for field in (U, V, W)]
            image = [s_ref[field, 0, at, :] for field in (HU, HV, HW)]
            second = [shifted(field, 0, r) for field in (HU, HV, HW)]
            for left, right in ((fields, fields), (fields, image), (image, image), (image, second)):
                new += [left[i] * right[j] for i, j in PAIRS]
            return tuple(s + n for s, n in zip(sums, new))

        zero = jnp.zeros((8, LANES), jnp.float32)
        sums = lax.fori_loop(1, CHUNKS - 1, gather, (zero,) * NSUMS, unroll=True)
        line = jnp.zeros((1, LANES), jnp.float32)
        for index, value in enumerate(sums):
            total = jnp.sum(jnp.sum(value, axis=1, keepdims=True), axis=0, keepdims=True)
            line = jnp.where(lane[0:1, :] == index, total, line)
        sums_ref[...] = jnp.broadcast_to(line, (devices, LANES))

        def hand_over(r, carry):
            at = rows_at(r)
            out_at = pl.ds(pl.multiple_of(8 * r, 8), 8)
            for slot, field in enumerate((B, H, U, V, W, HU, HV, HW, DEP)):
                f_out_ref[slot, out_at, :] = s_ref[field, 0, at, :]
            for slot, field in enumerate((U, V, W, HU, HV, HW, DEP)):
                z_out_ref[3 + slot, out_at, :] = jnp.where(inner, s_ref[field, 2, at, :], s_ref[field, 1, at, :])
            return carry

        lax.fori_loop(0, CHUNKS, hand_over, 0, unroll=True)

    return kernel


def solve(m0, m1, m2, m3):
    mean = m1 / m0
    theta = mean + SHIFT
    spread = m2 - mean * m1
    ratio = spread / (theta * theta * m0)
    curve = m3 - 2.0 * mean * m2 + mean * mean * m1 + SHIFT * spread
    gamma = curve / spread - ratio * theta
    image_factor = -1.0 / (theta * gamma)
    return 1.0 / theta + (mean / theta + ratio) / gamma, image_factor


def finish_kernel(c_ref, zon_ref, mer_ref, am_ref, pq_ref, f_ref, z_ref, sums_ref, out_ref, sens_ref, m_ref, x_ref):
    lane = lane_iota()
    group = lane // 8
    level_of = (group % 8).astype(jnp.float32)
    coup = [c_ref[level // 8, level % 8] for level in range(16)]
    coup_lane = jnp.zeros((8, LANES), jnp.float32)
    for level in range(16):
        coup_lane = jnp.where(group == level, coup[level], coup_lane)

    line = jnp.sum(sums_ref[...], axis=0, keepdims=True)

    def total(index):
        return jnp.sum(jnp.where(lane[0:1, :] == index, line, 0.0), axis=1, keepdims=True)

    a1, e1 = solve(*[total(i) for i in range(4)])
    y = (None, a1, e1)
    factor = (None, a1 * 2.0, e1 * 2.0, a1 * a1, a1 * e1 * 2.0, e1 * e1)
    moments = []
    for kind in range(4):
        base = 4 + kind * len(PAIRS)
        value = total(base)
        for index in range(1, len(PAIRS)):
            value = value + factor[index] * total(base + index)
        moments.append(value)
    a0, e0 = solve(*moments)
    a1, e1, a0, e0 = [jnp.broadcast_to(v, (8, LANES)) for v in (a1, e1, a0, e0)]
    FB, FH, FU, FV, FW, FHU, FHV, FHW, FDEP = range(9)
    ZAM, ZP, ZQ, ZU, ZV, ZW, ZHU, ZHV, ZHW, ZDEP = range(10)

    def middle(r, carry):
        at = pl.ds(pl.multiple_of(8 * r, 8), 8)
        to = pl.ds(pl.multiple_of(8 * r + HALO, 8), 8)
        b = f_ref[FU, at, :] + a1 * f_ref[FV, at, :] + e1 * f_ref[FW, at, :]
        h = f_ref[FHU, at, :] + a1 * f_ref[FHV, at, :] + e1 * f_ref[FHW, at, :]
        x = a0 * b + e0 * h
        x_ref[at, :] = x + a1 * f_ref[FB, at, :] + e1 * f_ref[FH, at, :]
        dep = f_ref[FDEP, at, :]
        for k in range(8):
            both = a1 * pq_ref[k, at, :] + e1 * pq_ref[8 + k, at, :] + jnp.where(dep > float(k), x, 0.0)
            for level in (k, k + 8):
                m_ref[level, to, :] = am_ref[level, at, :] + coup[level] * both
        return carry

    lax.fori_loop(0, CHUNKS, middle, 0, unroll=2)
    sens_ref[...] = x_ref[HALO : HALO + ROWS, :]

    for k in range(16):
        m_ref[k, 0:8, :] = jnp.zeros((8, LANES), jnp.float32)

    def west_east(main, z):
        return roll(jnp.where(lane == LANES - 1, z, main), 1), roll(jnp.where(lane == 0, z, main), -1)

    def advect(r, carry):
        at = pl.ds(pl.multiple_of(8 * r + HALO, 8), 8)
        out_at = pl.ds(pl.multiple_of(8 * r, 8), 8)
        start = 8 * r + 2 * HALO
        here = pl.ds(pl.multiple_of(start, 8), 8)
        below, above = pl.ds(start - 1, 8), pl.ds(start + 1, 8)
        zb = z_ref[ZU, at, :] + a1 * z_ref[ZV, at, :] + e1 * z_ref[ZW, at, :]
        zh = z_ref[ZHU, at, :] + a1 * z_ref[ZHV, at, :] + e1 * z_ref[ZHW, at, :]
        zx = a0 * zb + e0 * zh
        zd = z_ref[ZDEP, at, :]
        zm = z_ref[ZAM, at, :] + coup_lane * (
            a1 * z_ref[ZP, at, :] + e1 * z_ref[ZQ, at, :] + jnp.where(zd > level_of, zx, 0.0)
        )
        dep = f_ref[FDEP, at, :]
        dw, de = west_east(dep, roll(zd, -4))
        ds = f_ref[FDEP, pl.ds(8 * r + HALO - 1, 8), :]
        dn = f_ref[FDEP, pl.ds(8 * r + HALO + 1, 8), :]
        dw, de, ds, dn = [jnp.minimum(dep, d) for d in (dw, de, ds, dn)]
        for k in range(8):
            u = 0.5 * zon_ref[0, k, out_at, :].astype(jnp.float32)
            w = 0.5 * mer_ref[0, k, out_at, :].astype(jnp.float32)
            cw = jnp.where(dw > float(k), DIFF - u, 0.0)
            ce = jnp.where(de > float(k), DIFF + u, 0.0)
            cs = jnp.where(ds > float(k), DIFF - w, 0.0)
            cn = jnp.where(dn > float(k), DIFF + w, 0.0)
            c0 = 1.0 - ((cw + ce) + (cs + cn))
            for level in (k, k + 8):
                centre = m_ref[level, here, :]
                west, east = west_east(centre, roll(zm, -(8 * level + 4)))
                out_ref[level, out_at, :] = (
                    c0 * centre + cw * west + ce * east + cs * m_ref[level, below, :] + cn * m_ref[level, above, :]
                )
        return carry

    lax.fori_loop(0, ROWS // 8, advect, 0, unroll=2)


VMEM = pl.BlockSpec(memory_space=pltpu.VMEM)
HBM = pl.BlockSpec(memory_space=pltpu.HBM)


def on_device_of(lon, lat):
    devices = lon * lat
    f32 = jnp.float32

    def array(*shape):
        return jax.ShapeDtypeStruct(shape, f32)

    smem = pl.BlockSpec(memory_space=pltpu.SMEM)
    params = pltpu.CompilerParams(vmem_limit_bytes=48 * 2**20)
    pairs = {}
    for axis, count in (("lon", lon), ("lat", lat)):
        first = [(i, i ^ 1) for i in range(count)]
        second = [(i, (i - 1) % count if i % 2 == 0 else (i + 1) % count) for i in range(count)]
        pairs[axis] = (first, second)

    def swap(axis, a, b):
        first, second = pairs[axis]
        return lax.ppermute(a, axis, first), lax.ppermute(b, axis, second)

    def on_device(adj_tracer, zonal_flow, meridional_flow, depth, coupling, surface_diag):
        adj = adj_tracer.reshape(16, ROWS, LANES)
        block_args = (adj, zonal_flow, meridional_flow, depth, surface_diag)
        msg_a, msg_b = pl.pallas_call(
            row_message_kernel,
            in_specs=[HBM] * 5,
            out_specs=[VMEM] * 2,
            out_shape=[array(MSG_ROWS, LANES)] * 2,
            scratch_shapes=[
                pltpu.VMEM((2, 16, 8, LANES), f32),
                pltpu.VMEM((2, 2, 8, 8, LANES), jnp.bfloat16),
                pltpu.VMEM((2, 8, LANES), jnp.int32),
                pltpu.VMEM((2, 8, LANES), f32),
                pltpu.SemaphoreType.DMA((10,)),
            ],
            compiler_params=pltpu.CompilerParams(vmem_limit_bytes=62914560),
            name="row_messages",
        )(*block_args)
        recv_a, recv_b = swap("lat", msg_a, msg_b)
        row_scratch = [pltpu.VMEM((MSG_ROWS, LANES), f32)] * 2
        own = pl.pallas_call(
            make_pack_kernel(lat - 1),
            in_specs=[VMEM] * 7,
            out_specs=VMEM,
            out_shape=array(3 * EXT, LANES),
            scratch_shapes=row_scratch,
            compiler_params=params,
            name="pack_columns",
        )(*block_args, recv_a, recv_b)
        side_a, side_b = swap("lon", own, own)
        outs = [(16, EXT, LANES), (16, EXT, LANES), (9, EXT, LANES), (10, EXT, LANES), (devices, LANES)]
        am, pq, fields, zs, sums = pl.pallas_call(
            make_fields_kernel(lat - 1, devices),
            in_specs=[smem] + [VMEM] * 10,
            out_specs=[VMEM] * 5,
            out_shape=[array(*s) for s in outs],
            scratch_shapes=row_scratch
            + [
                pltpu.VMEM((16, PAD, LANES), f32),
                pltpu.VMEM((16, PAD, LANES), f32),
                pltpu.VMEM((10, 3, PAD, LANES), f32),
                pltpu.VMEM((2, PAD, LANES), f32),
                pltpu.VMEM((2, PAD, LANES), f32),
            ],
            compiler_params=params,
            name="fields",
        )(coupling, *block_args, recv_a, recv_b, own, side_a, side_b)
        everyone = lax.all_to_all(sums, ("lon", "lat"), 0, 0, tiled=True)
        out, sens = pl.pallas_call(
            finish_kernel,
            in_specs=[smem] + [VMEM] * 7,
            out_specs=[VMEM] * 2,
            out_shape=[array(16, ROWS, LANES), array(ROWS, LANES)],
            scratch_shapes=[pltpu.VMEM((16, PAD, LANES), f32), pltpu.VMEM((EXT, LANES), f32)],
            compiler_params=params,
            name="finish",
        )(coupling, zonal_flow, meridional_flow, am, pq, fields, zs, everyone)
        return out.reshape(adj_tracer.shape), sens

    return on_device


def solution(mesh):
    in_specs = (
        P(None, None, "lat", "lon"),
        P(None, None, "lat", "lon"),
        P(None, None, "lat", "lon"),
        P("lat", "lon"),
        P(),
        P("lat", "lon"),
    )
    out_specs = (P(None, None, "lat", "lon"), P("lat", "lon"))
    return jax.shard_map(
        on_device_of(mesh.shape["lon"], mesh.shape["lat"]),
        mesh=mesh, in_specs=in_specs, out_specs=out_specs, check_vma=False,
    )
```

```python
import jax
import jax.numpy as jnp
from jax import lax
from jax.experimental import pallas as pl
from jax.experimental.pallas import tpu as pltpu
from jax.sharding import PartitionSpec as P

DIFF = 0.15
SHIFT = 4.0
LANES = 128
ROWS = 64
HALO = 8
EXT = ROWS + 2 * HALO
PAD = EXT + 2 * HALO
CHUNKS = EXT // 8
FLOW_AT, MASK_AT, DEPTH_AT, DIAG_AT, MSG_ROWS = 8, 40, 104, 108, 120
DEP, DIA, B, H, U, V, W, HU, HV, HW = range(10)
M0, M1, FU, FV, PDEP, PDIA = range(6)
FIRST, LAST = 4, LANES - 5
PAIRS = ((0, 0), (0, 1), (0, 2), (1, 1), (1, 2), (2, 2))
NSUMS = 5 + 5 * len(PAIRS)
SUM_ROWS = 40


def lane_iota():
    return lax.broadcasted_iota(jnp.int32, (8, LANES), 1)


def roll(x, by):
    by = by % LANES
    return pltpu.roll(x, by, 1) if by else x


def over_groups(x):
    for by in (16, 32, 64):
        x = x + roll(x, by)
    return x


def in_every_group(x, lane):
    return over_groups(jnp.where(lane < 16, x, 0.0))


def message_shift(level):
    return 16 * (level % 8) + 8 * (level // 8) + 4


def own_shift(level):
    return 16 * (level % 8) + 8


def pack_messages(values, lane):
    eighth = lane // 8
    packed = values[0]
    for level, value in enumerate(values):
        turned = roll(value, message_shift(level))
        packed = jnp.where(eighth == 2 * (level % 8) + level // 8, turned, packed) if level else turned
    return packed


def pack_own(values, lane):
    packed = roll(values[0], own_shift(0))
    for level in range(1, 8):
        packed = jnp.where(lane // 16 == level, roll(values[level], own_shift(level)), packed)
    return packed


def pack_surface(depth, diag, lane):
    return in_every_group(jnp.where(lane % 16 < 8, roll(depth, 4), roll(diag, 12)), lane)


def aligned(start, count=8):
    return pl.ds(pl.multiple_of(start, 8), count)


def level_rows(ref, at, count, index, south):
    start = at + count * index
    return ref[pl.ds(start - (8 - count) if south else start, 8), :]


def row_message_kernel(adj, zon, mer, depth, diag, a_ref, b_ref, adj_ref, flow_ref, depth_ref, diag_ref, sems):
    copies = []
    for edge, start in ((0, 0), (1, ROWS - 8)):
        rows = pl.ds(start, 8)
        for source, target in (
            (adj.at[:, rows, :], adj_ref.at[edge]),
            (zon.at[1, :, rows, :], flow_ref.at[edge, 0]),
            (mer.at[1, :, rows, :], flow_ref.at[edge, 1]),
            (depth.at[rows, :], depth_ref.at[edge]),
            (diag.at[rows, :], diag_ref.at[edge]),
        ):
            copies.append(pltpu.make_async_copy(source, target, sems.at[len(copies)]))
            copies[-1].start()
    even = lax.rem(lax.axis_index("lat"), 2) == 0
    zero = jnp.zeros((8, LANES), jnp.float32)
    for ref in (a_ref, b_ref):
        ref[0:8, :] = zero
        ref[MSG_ROWS - 8 : MSG_ROWS, :] = zero
    for copy in copies:
        copy.wait()

    def put(at, low, high):
        count = low.shape[0]
        a_ref[pl.ds(at, count), :] = jnp.where(even, high, low)
        b_ref[pl.ds(at, count), :] = jnp.where(even, low, high)

    depth_low = depth_ref[0, 0:4, :].astype(jnp.float32)
    depth_high = depth_ref[1, 4:8, :].astype(jnp.float32)
    for level in range(16):
        k = float(level % 8)
        low = jnp.where(depth_low > k, adj_ref[0, level, 0:4, :], 0.0)
        high = jnp.where(depth_high > k, adj_ref[1, level, 4:8, :], 0.0)
        put(MASK_AT + 4 * level, low, high)
    put(DEPTH_AT, depth_low, depth_high)
    put(DIAG_AT, diag_ref[0, 0:4, :], diag_ref[1, 4:8, :])
    for level in range(16):
        low = 0.5 * flow_ref[0, level // 8, level % 8].astype(jnp.float32)
        high = 0.5 * flow_ref[1, level // 8, level % 8].astype(jnp.float32)
        put(FLOW_AT + 2 * level, low[0:2], high[6:8])


def sort_rows(recv_a_ref, recv_b_ref, south_ref, north_ref, last):
    lat = lax.axis_index("lat")
    even = lax.rem(lat, 2) == 0
    for start in range(0, MSG_ROWS, 8):
        a = recv_a_ref[pl.ds(start, 8), :]
        b = recv_b_ref[pl.ds(start, 8), :]
        south_ref[pl.ds(start, 8), :] = jnp.where(lat == 0, 0.0, jnp.where(even, b, a))
        north_ref[pl.ds(start, 8), :] = jnp.where(lat == last, 0.0, jnp.where(even, a, b))


def pack_interior_kernel(c_ref, adj_ref, zon_ref, mer_ref, depth_ref, diag_ref, o_ref, own_ref, late_ref, m_ref, f_ref):
    del c_ref
    lane = lane_iota()

    def rows(r, carry):
        at = aligned(8 * r)
        to = aligned(8 * r + HALO)
        depth = depth_ref[at, :].astype(jnp.float32)
        diag = diag_ref[at, :]
        masked = [jnp.where(depth > float(level % 8), adj_ref[level, at, :], 0.0) for level in range(16)]
        flows = [
            0.5 * ref[1, k, at, :].astype(jnp.float32) for ref in (zon_ref, mer_ref) for k in range(8)
        ]
        for level in range(16):
            m_ref[level, aligned(8 * r + 2 * HALO), :] = masked[level]
            f_ref[level, aligned(8 * r + 2 * HALO), :] = flows[level]
        o_ref[to, :] = pack_messages(masked, lane)
        o_ref[aligned(EXT + 8 * r + HALO), :] = pack_messages(flows, lane)
        o_ref[aligned(2 * EXT + 8 * r + HALO), :] = pack_surface(depth, diag, lane)
        own_ref[M0, to, :] = pack_own(masked[:8], lane)
        own_ref[M1, to, :] = pack_own(masked[8:], lane)
        own_ref[FU, to, :] = pack_own(flows[:8], lane)
        own_ref[FV, to, :] = pack_own(flows[8:], lane)
        own_ref[PDEP, to, :] = in_every_group(roll(depth, 8), lane)
        own_ref[PDIA, to, :] = in_every_group(roll(diag, 8), lane)
        for which, ref in enumerate((zon_ref, mer_ref)):
            late_ref[which, at, :] = pack_own([0.5 * ref[0, k, at, :].astype(jnp.float32) for k in range(8)], lane)
        return carry

    lax.fori_loop(0, ROWS // 8, rows, 0)


def make_pack_edges_kernel(last):
    def kernel(ra_ref, rb_ref, o_in_ref, o_ref, south_ref, north_ref):
        del o_in_ref
        sort_rows(ra_ref, rb_ref, south_ref, north_ref, last)
        lane = lane_iota()
        for ref, south, base in ((south_ref, True, 0), (north_ref, False, HALO + ROWS)):
            masked = [level_rows(ref, MASK_AT, 4, level, south) for level in range(16)]
            o_ref[base : base + 8, :] = pack_messages(masked, lane)
            flows = [level_rows(ref, FLOW_AT, 2, level, south) for level in range(16)]
            o_ref[EXT + base : EXT + base + 8, :] = pack_messages(flows, lane)
            depth = level_rows(ref, DEPTH_AT, 4, 0, south)
            diag = level_rows(ref, DIAG_AT, 4, 0, south)
            o_ref[2 * EXT + base : 2 * EXT + base + 8, :] = pack_surface(depth, diag, lane)

    return kernel


def rows_at(r, shift=0):
    start = HALO + 8 * r
    return pl.ds(pl.multiple_of(start, 8) if shift == 0 else start + shift, 8)


def star(ref, r):
    centre = ref[rows_at(r), :]
    return centre, roll(centre, 1), roll(centre, -1), ref[rows_at(r, -1), :], ref[rows_at(r, 1), :]


def shifted(ref, diag_ref, r):
    centre, west, east, south, north = star(ref, r)
    return diag_ref[rows_at(r), :] * centre - (west + east + south + north)


def on_grid(r, last, value):
    lat = lax.axis_index("lat")
    at = 8 * r + lax.broadcasted_iota(jnp.int32, (8, LANES), 0) - HALO
    beyond = ((at < 0) & (lat == 0)) | ((at >= ROWS) & (lat == last))
    return jnp.where(beyond, 0.0, value)


def apply(coef, centre, west, east, south, north):
    c0, cw, ce, cs, cn = coef
    return (c0 * centre + cw * west) + (ce * east + cs * south) + cn * north


def coefficients(u, w, mins, k):
    dep, dw, de, ds, dn = mins
    cw = jnp.where(dw > k, DIFF - u, 0.0)
    ce = jnp.where(de > k, DIFF + u, 0.0)
    cs = jnp.where(ds > k, DIFF - w, 0.0)
    cn = jnp.where(dn > k, DIFF + w, 0.0)
    c0 = jnp.where(dep > k, 1.0 - ((cw + ce) + (cs + cn)), 0.0)
    return c0, cw, ce, cs, cn


def depths(ref, r):
    dep, *others = star(ref, r)
    return [dep] + [jnp.minimum(dep, d) for d in others]


def products(b, h, hh, fields, image, second):
    new = [b * b, b * h, h * h, h * hh, b * hh]
    for left, right in ((fields, fields), (fields, image), (image, image), (image, second), (fields, second)):
        for i, j in PAIRS:
            if i == j or left is right:
                new.append(left[i] * right[j])
            else:
                new.append(left[i] * right[j] + left[j] * right[i])
    return new


def make_block_kernel(last):
    def kernel(
        c_ref, depth_ref, diag_ref, ra_ref, rb_ref, own_in_ref, m_in_ref, f_in_ref,
        am_ref, pq_ref, s_ref, sums_ref, shift_ref, own_ref, m_ref, f_ref,
        south_ref, north_ref,
    ):
        del own_in_ref, m_in_ref, f_in_ref
        lane = lane_iota()
        coup = [c_ref[level // 8, level % 8] for level in range(16)]
        square = [coup[k] * coup[k] + coup[k + 8] * coup[k + 8] for k in range(8)]
        sort_rows(ra_ref, rb_ref, south_ref, north_ref, last)
        lo, hi, mid = HALO, EXT, 2 * HALO
        for level in range(16):
            for ref, at, count in ((m_ref, MASK_AT, 4), (f_ref, FLOW_AT, 2)):
                ref[level, lo : lo + 8, :] = level_rows(south_ref, at, count, level, True)
                ref[level, hi : hi + 8, :] = level_rows(north_ref, at, count, level, False)
        for field, at in ((DEP, DEPTH_AT), (DIA, DIAG_AT)):
            s_ref[field, lo : lo + 8, :] = level_rows(south_ref, at, 4, 0, True)
            s_ref[field, hi : hi + 8, :] = level_rows(north_ref, at, 4, 0, False)

        s_ref[DEP, mid : mid + ROWS, :] = depth_ref[...].astype(jnp.float32)
        s_ref[DIA, mid : mid + ROWS, :] = diag_ref[...]

        def rhs(r, carry):
            at = rows_at(r)
            parts = [coup[level] * m_ref[level, at, :] for level in range(16)]
            while len(parts) > 1:
                parts = [parts[i] + parts[i + 1] for i in range(0, len(parts), 2)]
            s_ref[B, at, :] = parts[0]
            return carry

        lax.fori_loop(0, CHUNKS, rhs, 0)

        zero = jnp.zeros((8, LANES), jnp.float32)

        def quotient(r, carry):
            b = s_ref[B, rows_at(r), :]
            return carry[0] + b * b, carry[1] + b * shifted(s_ref.at[B], s_ref.at[DIA], r)

        squares, images_sum = lax.fori_loop(1, CHUNKS - 1, quotient, (zero, zero), unroll=2)
        inside = (lane > 0) & (lane < LANES - 1)
        squares, images_sum = [
            jnp.sum(jnp.sum(jnp.where(inside, v, 0.0), axis=0, keepdims=True), axis=1, keepdims=True)
            for v in (squares, images_sum)
        ]
        shift = jnp.where(squares > 0.0, images_sum / jnp.where(squares > 0.0, squares, 1.0), 0.0)
        shift = jnp.broadcast_to(jnp.clip(shift, -4.0, 5.0), (8, LANES))
        shift_ref[...] = shift

        def images(r, carry):
            s_ref[DIA, rows_at(r), :] = s_ref[DIA, rows_at(r), :] - shift
            s_ref[H, rows_at(r), :] = on_grid(r, last, shifted(s_ref.at[B], s_ref.at[DIA], r))
            return carry

        lax.fori_loop(0, CHUNKS, images, 0, unroll=2)

        def advect(r, carry):
            out_at = aligned(8 * r)
            at, below, above = rows_at(r), rows_at(r, -1), rows_at(r, 1)
            mins = depths(s_ref.at[DEP], r)
            bs = star(s_ref.at[B], r)
            hs = star(s_ref.at[H], r)
            us = vs = ws = jnp.zeros((8, LANES), jnp.float32)
            for k in range(8):
                coef = coefficients(f_ref[k, at, :], f_ref[8 + k, at, :], mins, float(k))
                for level in (k, k + 8):
                    centre = m_ref[level, at, :]
                    value = apply(
                        coef, centre, roll(centre, 1), roll(centre, -1),
                        m_ref[level, below, :], m_ref[level, above, :],
                    )
                    am_ref[level, out_at, :] = value
                    us = us + coup[level] * value
                p = apply(coef, *bs)
                q = apply(coef, *hs)
                pq_ref[k, out_at, :] = p
                pq_ref[8 + k, out_at, :] = q
                vs = vs + square[k] * p
                ws = ws + square[k] * q
            s_ref[U, at, :] = us
            s_ref[V, at, :] = vs
            s_ref[W, at, :] = ws
            return carry

        lax.fori_loop(0, CHUNKS, advect, 0)

        def images_two(r, carry):
            for source, target in ((U, HU), (V, HV), (W, HW)):
                s_ref[target, rows_at(r), :] = on_grid(r, last, shifted(s_ref.at[source], s_ref.at[DIA], r))
            return carry

        lax.fori_loop(0, CHUNKS, images_two, 0, unroll=2)

        def gather(r, sums):
            at = rows_at(r)
            hh, *second = [shifted(s_ref.at[field], s_ref.at[DIA], r) for field in (H, HU, HV, HW)]
            b, h, *rest = [s_ref[field, at, :] for field in (B, H, U, V, W, HU, HV, HW)]
            return tuple(s + n for s, n in zip(sums, products(b, h, hh, rest[:3], rest[3:], second)))

        sums = lax.fori_loop(1, CHUNKS - 1, gather, (zero,) * NSUMS)
        keep = (lane >= FIRST) & (lane <= LAST)
        for index, value in enumerate(sums):
            sums_ref[8 * index : 8 * index + 8, :] = jnp.where(keep, value, 0.0)

        for ref, south, base in ((south_ref, True, 0), (north_ref, False, HALO + ROWS)):
            rows = pl.ds(base, 8)
            for slot, at, count in ((M0, MASK_AT, 4), (FU, FLOW_AT, 2)):
                values = [level_rows(ref, at, count, level, south) for level in range(16)]
                own_ref[slot, rows, :] = pack_own(values[:8], lane)
                own_ref[slot + 1, rows, :] = pack_own(values[8:], lane)
            for slot, at in ((PDEP, DEPTH_AT), (PDIA, DIAG_AT)):
                own_ref[slot, rows, :] = in_every_group(roll(level_rows(ref, at, 4, 0, south), 8), lane)

    return kernel


def group_factors(c_ref, lane):
    first = second = jnp.zeros((8, LANES), jnp.float32)
    for k in range(8):
        first = jnp.where(lane // 16 == k, c_ref[0, k], first)
        second = jnp.where(lane // 16 == k, c_ref[1, k], second)
    return first, second


def make_sides_kernel(last, devices):
    def kernel(
        c_ref, own_ref, pa_ref, pb_ref, block_sums_ref, shift_ref, z_ref, s_ref, sums_ref, m_ref, f_ref, all_ref
    ):
        lane = lane_iota()
        pos = lane % 16
        level_of = (lane // 16).astype(jnp.float32)
        first, second = group_factors(c_ref, lane)
        square = first * first + second * second
        even_lon = lax.rem(lax.axis_index("lon"), 2) == 0
        shift = shift_ref[...]

        def assemble(r, carry):
            at = rows_at(r)
            own_at = aligned(8 * r)
            for side in range(2):
                outer = pos >= 8 if side == 0 else pos < 8
                for part in range(3):
                    src = aligned(part * EXT + 8 * r)
                    a, b = pa_ref[src, :], pb_ref[src, :]
                    got = jnp.where(even_lon, a, b) if side == 0 else jnp.where(even_lon, b, a)
                    one = jnp.where(outer, roll(got, 4), own_ref[2 * part, own_at, :])
                    two = jnp.where(outer, roll(got, -4), own_ref[2 * part + 1, own_at, :])
                    if part == 0:
                        m_ref[side, 0, at, :] = one
                        m_ref[side, 1, at, :] = two
                        s_ref[side, B, at, :] = over_groups(first * one + second * two)
                    elif part == 1:
                        f_ref[side, 0, at, :] = one
                        f_ref[side, 1, at, :] = two
                    else:
                        s_ref[side, DEP, at, :] = one
                        s_ref[side, DIA, at, :] = two - shift
            return carry

        lax.fori_loop(0, CHUNKS, assemble, 0, unroll=10)

        def images(r, carry):
            for side in range(2):
                value = shifted(s_ref.at[side, B], s_ref.at[side, DIA], r)
                s_ref[side, H, rows_at(r), :] = on_grid(r, last, value)
            return carry

        lax.fori_loop(0, CHUNKS, images, 0, unroll=10)

        def advect(r, carry):
            at, out_at = rows_at(r), aligned(8 * r)
            for side in range(2):
                mins = depths(s_ref.at[side, DEP], r)
                coef = coefficients(f_ref[side, 0, at, :], f_ref[side, 1, at, :], mins, level_of)
                one = apply(coef, *star(m_ref.at[side, 0], r))
                two = apply(coef, *star(m_ref.at[side, 1], r))
                p = apply(coef, *star(s_ref.at[side, B], r))
                q = apply(coef, *star(s_ref.at[side, H], r))
                for slot, value in enumerate((one, two, p, q)):
                    z_ref[side, slot, out_at, :] = value
                s_ref[side, U, at, :] = over_groups(first * one + second * two)
                s_ref[side, V, at, :] = over_groups(square * p)
                s_ref[side, W, at, :] = over_groups(square * q)
            return carry

        lax.fori_loop(0, CHUNKS, advect, 0, unroll=5)

        def images_two(r, carry):
            for side in range(2):
                for source, target in ((U, HU), (V, HV), (W, HW)):
                    value = shifted(s_ref.at[side, source], s_ref.at[side, DIA], r)
                    s_ref[side, target, rows_at(r), :] = on_grid(r, last, value)
            return carry

        lax.fori_loop(0, CHUNKS, images_two, 0, unroll=5)

        east = lane < 8

        def gather(r, sums):
            at = rows_at(r)

            def both(field):
                return jnp.where(east, s_ref[0, field, at, :], s_ref[1, field, at, :])

            def image(field):
                one, two = [shifted(s_ref.at[side, field], s_ref.at[side, DIA], r) for side in range(2)]
                return jnp.where(east, one, two)

            hh, *second_image = [image(field) for field in (H, HU, HV, HW)]
            b, h, *rest = [both(field) for field in (B, H, U, V, W, HU, HV, HW)]
            return tuple(s + n for s, n in zip(sums, products(b, h, hh, rest[:3], rest[3:], second_image)))

        zero = jnp.zeros((8, LANES), jnp.float32)
        sums = lax.fori_loop(1, CHUNKS - 1, gather, (zero,) * NSUMS, unroll=1)
        keep = (lane >= 4) & (lane < 12)
        for index, value in enumerate(sums):
            at = pl.ds(8 * index, 8)
            all_ref[at, :] = block_sums_ref[at, :] + jnp.where(keep, value, 0.0)
        for index in range(NSUMS, SUM_ROWS):
            all_ref[pl.ds(8 * index, 8), :] = zero
        row = lax.broadcasted_iota(jnp.int32, (8, LANES), 0)
        line = jnp.zeros((8, LANES), jnp.float32)
        for base in range(0, SUM_ROWS, 8):
            total = all_ref[pl.ds(8 * base, 8, stride=8), :]
            for sub in range(1, 8):
                total = total + all_ref[pl.ds(8 * base + sub, 8, stride=8), :]
            total = jnp.sum(total, axis=1, keepdims=True)
            line = jnp.where(lane == base + row, total, line)
        line = jnp.sum(line, axis=0, keepdims=True)
        line = jnp.where(lane[0:1, :] == NSUMS, shift[0:1, :], line)
        sums_ref[...] = jnp.broadcast_to(line, (devices, LANES))

    return kernel


def solve(m0, m1, m2, m3, m4, shift):
    def over_devices(x):
        return jnp.sum(x, axis=1, keepdims=True)

    norm = over_devices(m0)
    mean = over_devices(m1 + shift * m0) / norm
    theta = mean + SHIFT
    delta = shift - mean
    spread = over_devices(m2 + delta * (2.0 * m1 + delta * m0))
    curve = over_devices(m3 + delta * (2.0 * m2 + m4 + delta * (3.0 * m1 + delta * m0)))
    ratio = spread / (theta * theta * norm)
    gamma = curve / spread + theta * (1.0 - ratio)
    image = -1.0 / (theta * gamma)
    return 1.0 / theta + ratio / gamma + delta * image, image


def make_finish_kernel(lat_count):
    def kernel(
        c_ref, zon_ref, mer_ref, am_ref, pq_ref, s_ref, late_ref, z_ref, side_ref, sums_ref,
        out_ref, sens_ref, m_ref, zm_ref, zx_ref,
    ):
        lane = lane_iota()
        pos = lane % 16
        level_of = (lane // 16).astype(jnp.float32)
        coup = [c_ref[level // 8, level % 8] for level in range(16)]
        first, second = group_factors(c_ref, lane)

        devices = sums_ref.shape[0]
        blocks = []
        for base in range(0, devices, LANES):
            part = sums_ref[base : min(base + LANES, devices), :]
            if part.shape[0] < LANES:
                part = jnp.concatenate([part, jnp.zeros((LANES - part.shape[0], LANES), jnp.float32)], axis=0)
            blocks.append(jnp.transpose(part))
        turned = blocks[0] if len(blocks) == 1 else jnp.concatenate(blocks, axis=1)
        rows = [turned[i : i + 1, :] for i in range(NSUMS + 1)]
        shift = rows[NSUMS]
        near, e1 = solve(*rows[:5], shift)
        factor = (None, near, e1, near * near, near * e1, e1 * e1)
        moments = []
        for kind in range(5):
            base = 5 + kind * len(PAIRS)
            value = rows[base]
            for index in range(1, len(PAIRS)):
                twice = 2.0 if kind in (0, 2) and index in (1, 2, 4) else 1.0
                value = value + (twice * factor[index]) * rows[base + index]
            moments.append(value)
        late, e0 = solve(*moments, shift)
        me = lax.axis_index("lon") * lat_count + lax.axis_index("lat")
        mine = lax.broadcasted_iota(jnp.int32, shift.shape, 1) == me
        a1, a0 = [jnp.sum(jnp.where(mine, v, 0.0), axis=1, keepdims=True) for v in (near, late)]
        a1, e1, a0, e0 = [jnp.broadcast_to(v, (8, LANES)) for v in (a1, e1, a0, e0)]

        def surface(ref, at):
            b = ref[U, at, :] + a1 * ref[V, at, :] + e1 * ref[W, at, :]
            h = ref[HU, at, :] + a1 * ref[HV, at, :] + e1 * ref[HW, at, :]
            x = a0 * b + e0 * h
            return x, x + (a1 * ref[B, at, :] + e1 * ref[H, at, :])

        def middle(r, carry):
            at, to = aligned(8 * r), rows_at(r)
            for side in range(2):
                x, both_steps = surface(side_ref.at[side], to)
                zx_ref[side, at, :] = both_steps
                part = a1 * z_ref[side, 2, at, :] + e1 * z_ref[side, 3, at, :]
                part = part + jnp.where(side_ref[side, DEP, to, :] > level_of, x, 0.0)
                zm_ref[side, 0, to, :] = z_ref[side, 0, at, :] + first * part
                zm_ref[side, 1, to, :] = z_ref[side, 1, at, :] + second * part
            x, both_steps = surface(s_ref, to)
            zx_ref[2, at, :] = both_steps
            dep = s_ref[DEP, to, :]
            for k in range(8):
                part = a1 * pq_ref[k, at, :] + e1 * pq_ref[8 + k, at, :] + jnp.where(dep > float(k), x, 0.0)
                for level in (k, k + 8):
                    m_ref[level, to, :] = am_ref[level, at, :] + coup[level] * part
            return carry

        lax.fori_loop(0, CHUNKS, middle, 0, unroll=2)

        edge = (lane < FIRST) | (lane > LAST)

        def advect(i, carry):
            r = i + 1
            out_at = aligned(8 * i)
            ext_at = aligned(8 * r)
            at, below, above = rows_at(r), rows_at(r, -1), rows_at(r, 1)
            sides = []
            for side in range(2):
                mins = depths(side_ref.at[side, DEP], r)
                coef = coefficients(late_ref[0, out_at, :], late_ref[1, out_at, :], mins, level_of)
                sides.append([apply(coef, *star(zm_ref.at[side, t], r)) for t in range(2)])
            inserts = [jnp.where(pos < 8, sides[0][t], sides[1][t]) for t in range(2)]
            ins = jnp.where(pos < 8, zx_ref[0, ext_at, :], zx_ref[1, ext_at, :])
            sens_ref[out_at, :] = jnp.where(edge, roll(ins, -8), zx_ref[2, ext_at, :])
            mins = depths(s_ref.at[DEP], r)
            for k in range(8):
                u = 0.5 * zon_ref[0, k, out_at, :].astype(jnp.float32)
                w = 0.5 * mer_ref[0, k, out_at, :].astype(jnp.float32)
                coef = coefficients(u, w, mins, float(k))
                for level in (k, k + 8):
                    centre = m_ref[level, at, :]
                    value = apply(
                        coef, centre, roll(centre, 1), roll(centre, -1),
                        m_ref[level, below, :], m_ref[level, above, :],
                    )
                    value = jnp.where(edge, roll(inserts[level // 8], -own_shift(k)), value)
                    out_ref[level, out_at, :] = value
            return carry

        lax.fori_loop(0, ROWS // 8, advect, 0, unroll=2)

    return kernel


VMEM = pl.BlockSpec(memory_space=pltpu.VMEM)
HBM = pl.BlockSpec(memory_space=pltpu.HBM)


def on_device_of(lon, lat):
    devices = lon * lat
    f32 = jnp.float32

    def array(*shape):
        return jax.ShapeDtypeStruct(shape, f32)

    smem = pl.BlockSpec(memory_space=pltpu.SMEM)
    params = pltpu.CompilerParams(vmem_limit_bytes=48 * 2**20)
    pairs = {}
    for axis, count in (("lon", lon), ("lat", lat)):
        first = [(i, i ^ 1) for i in range(count)]
        second = [(i, (i - 1) % count if i % 2 == 0 else (i + 1) % count) for i in range(count)]
        pairs[axis] = (first, second)

    def swap(axis, a, b):
        first, second = pairs[axis]
        return lax.ppermute(a, axis, first), lax.ppermute(b, axis, second)

    def on_device(adj_tracer, zonal_flow, meridional_flow, depth, coupling, surface_diag):
        adj = adj_tracer.reshape(16, ROWS, LANES)
        block_args = (adj, zonal_flow, meridional_flow, depth, surface_diag)
        msg_a, msg_b = pl.pallas_call(
            row_message_kernel,
            in_specs=[HBM] * 5,
            out_specs=[VMEM] * 2,
            out_shape=[array(MSG_ROWS, LANES)] * 2,
            scratch_shapes=[
                pltpu.VMEM((2, 16, 8, LANES), f32),
                pltpu.VMEM((2, 2, 8, 8, LANES), jnp.bfloat16),
                pltpu.VMEM((2, 8, LANES), jnp.int32),
                pltpu.VMEM((2, 8, LANES), f32),
                pltpu.SemaphoreType.DMA((10,)),
            ],
            compiler_params=pltpu.CompilerParams(vmem_limit_bytes=62914560),
            name="row_messages",
        )(*block_args)
        recv_a, recv_b = swap("lat", msg_a, msg_b)
        packed, own, late, masked, flows = pl.pallas_call(
            pack_interior_kernel,
            in_specs=[smem] + [VMEM] * 5,
            out_specs=[VMEM] * 5,
            out_shape=[
                array(3 * EXT, LANES), array(6, EXT, LANES), array(2, ROWS, LANES),
                array(16, PAD, LANES), array(16, PAD, LANES),
            ],
            compiler_params=params,
            cost_estimate=pl.CostEstimate(flops=4_000_000, bytes_accessed=1_000_000, transcendentals=0),
            name="pack_interior",
        )(coupling, *block_args)
        row_scratch = [pltpu.VMEM((MSG_ROWS, LANES), f32)] * 2
        packed = pl.pallas_call(
            make_pack_edges_kernel(lat - 1),
            in_specs=[VMEM] * 3,
            out_specs=VMEM,
            out_shape=array(3 * EXT, LANES),
            scratch_shapes=row_scratch,
            input_output_aliases={2: 0},
            compiler_params=params,
            name="pack_edges",
        )(recv_a, recv_b, packed)
        side_a, side_b = swap("lon", packed, packed)
        am, pq, block, block_sums, shift, own, _, _ = pl.pallas_call(
            make_block_kernel(lat - 1),
            in_specs=[smem] + [VMEM] * 7,
            out_specs=[VMEM] * 8,
            out_shape=[
                array(16, EXT, LANES), array(16, EXT, LANES), array(10, PAD, LANES),
                array(8 * NSUMS, LANES), array(8, LANES), array(6, EXT, LANES),
                array(16, PAD, LANES), array(16, PAD, LANES),
            ],
            scratch_shapes=row_scratch,
            input_output_aliases={5: 5, 6: 6, 7: 7},
            compiler_params=params,
            cost_estimate=pl.CostEstimate(flops=16_000_000, bytes_accessed=4_000_000, transcendentals=0),
            name="block",
        )(coupling, depth, surface_diag, recv_a, recv_b, own, masked, flows)
        z, sides, sums = pl.pallas_call(
            make_sides_kernel(lat - 1, devices),
            in_specs=[smem] + [VMEM] * 5,
            out_specs=[VMEM] * 3,
            out_shape=[array(2, 4, EXT, LANES), array(2, 10, PAD, LANES), array(devices, LANES)],
            scratch_shapes=[
                pltpu.VMEM((2, 2, PAD, LANES), f32),
                pltpu.VMEM((2, 2, PAD, LANES), f32),
                pltpu.VMEM((8 * SUM_ROWS, LANES), f32),
            ],
            compiler_params=params,
            name="sides",
        )(coupling, own, side_a, side_b, block_sums, shift)
        everyone = lax.all_to_all(sums, ("lon", "lat"), 0, 0, tiled=True)
        out, sens = pl.pallas_call(
            make_finish_kernel(lat),
            in_specs=[smem] + [VMEM] * 9,
            out_specs=[VMEM] * 2,
            out_shape=[array(16, ROWS, LANES), array(ROWS, LANES)],
            scratch_shapes=[
                pltpu.VMEM((16, PAD, LANES), f32),
                pltpu.VMEM((2, 2, PAD, LANES), f32),
                pltpu.VMEM((3, EXT, LANES), f32),
            ],
            compiler_params=params,
            name="finish",
        )(coupling, zonal_flow, meridional_flow, am, pq, block, late, z, sides, everyone)
        return out.reshape(adj_tracer.shape), sens

    return on_device


def solution(mesh):
    in_specs = (
        P(None, None, "lat", "lon"),
        P(None, None, "lat", "lon"),
        P(None, None, "lat", "lon"),
        P("lat", "lon"),
        P(),
        P("lat", "lon"),
    )
    out_specs = (P(None, None, "lat", "lon"), P("lat", "lon"))
    return jax.shard_map(
        on_device_of(mesh.shape["lon"], mesh.shape["lat"]),
        mesh=mesh, in_specs=in_specs, out_specs=out_specs, check_vma=False,
    )
```

```python
import jax
import jax.numpy as jnp
from jax import lax
from jax.experimental import pallas as pl
from jax.experimental.pallas import tpu as pltpu
from jax.sharding import PartitionSpec as P

DIFF = 0.15
SHIFT = 4.0
LANES = 128
ROWS = 64
HALO = 8
EXT = ROWS + 2 * HALO
PAD = EXT + 2 * HALO
CHUNKS = EXT // 8
FLOW_AT, MASK_AT, DEPTH_AT, DIAG_AT, MSG_ROWS = 8, 40, 104, 108, 120
DEP, DIA, B, H, U, V, W, HU, HV, HW = range(10)
M0, M1, FU, FV, PDEP, PDIA = range(6)
FIRST, LAST = 4, LANES - 5
PAIRS = ((0, 0), (0, 1), (0, 2), (1, 1), (1, 2), (2, 2))
NSUMS = 5 + 5 * len(PAIRS)
SUM_ROWS = 40


def lane_iota():
    return lax.broadcasted_iota(jnp.int32, (8, LANES), 1)


def roll(x, by):
    by = by % LANES
    return pltpu.roll(x, by, 1) if by else x


def over_groups(x):
    for by in (16, 32, 64):
        x = x + roll(x, by)
    return x


def in_every_group(x, lane):
    return over_groups(jnp.where(lane < 16, x, 0.0))


def message_shift(level):
    return 16 * (level % 8) + 8 * (level // 8) + 4


def own_shift(level):
    return 16 * (level % 8) + 8


def pack_messages(values, lane):
    eighth = lane // 8
    packed = values[0]
    for level, value in enumerate(values):
        turned = roll(value, message_shift(level))
        packed = jnp.where(eighth == 2 * (level % 8) + level // 8, turned, packed) if level else turned
    return packed


def pack_own(values, lane):
    packed = roll(values[0], own_shift(0))
    for level in range(1, 8):
        packed = jnp.where(lane // 16 == level, roll(values[level], own_shift(level)), packed)
    return packed


def pack_surface(depth, diag, lane):
    return in_every_group(jnp.where(lane % 16 < 8, roll(depth, 4), roll(diag, 12)), lane)


def aligned(start, count=8):
    return pl.ds(pl.multiple_of(start, 8), count)


def level_rows(ref, at, count, index, south):
    start = at + count * index
    return ref[pl.ds(start - (8 - count) if south else start, 8), :]


def row_message_kernel(adj, zon, mer, depth, diag, a_ref, b_ref, adj_ref, flow_ref, depth_ref, diag_ref, sems):
    copies = []
    for edge, start in ((0, 0), (1, ROWS - 8)):
        rows = pl.ds(start, 8)
        for source, target in (
            (adj.at[:, rows, :], adj_ref.at[edge]),
            (zon.at[1, :, rows, :], flow_ref.at[edge, 0]),
            (mer.at[1, :, rows, :], flow_ref.at[edge, 1]),
            (depth.at[rows, :], depth_ref.at[edge]),
            (diag.at[rows, :], diag_ref.at[edge]),
        ):
            copies.append(pltpu.make_async_copy(source, target, sems.at[len(copies)]))
            copies[-1].start()
    even = lax.rem(lax.axis_index("lat"), 2) == 0
    zero = jnp.zeros((8, LANES), jnp.float32)
    for ref in (a_ref, b_ref):
        ref[0:8, :] = zero
        ref[MSG_ROWS - 8 : MSG_ROWS, :] = zero
    for copy in copies:
        copy.wait()

    def put(at, low, high):
        count = low.shape[0]
        a_ref[pl.ds(at, count), :] = jnp.where(even, high, low)
        b_ref[pl.ds(at, count), :] = jnp.where(even, low, high)

    depth_low = depth_ref[0, 0:4, :].astype(jnp.float32)
    depth_high = depth_ref[1, 4:8, :].astype(jnp.float32)
    for level in range(16):
        k = float(level % 8)
        low = jnp.where(depth_low > k, adj_ref[0, level, 0:4, :], 0.0)
        high = jnp.where(depth_high > k, adj_ref[1, level, 4:8, :], 0.0)
        put(MASK_AT + 4 * level, low, high)
    put(DEPTH_AT, depth_low, depth_high)
    put(DIAG_AT, diag_ref[0, 0:4, :], diag_ref[1, 4:8, :])
    for level in range(16):
        low = 0.5 * flow_ref[0, level // 8, level % 8].astype(jnp.float32)
        high = 0.5 * flow_ref[1, level // 8, level % 8].astype(jnp.float32)
        put(FLOW_AT + 2 * level, low[0:2], high[6:8])


def sort_rows(recv_a_ref, recv_b_ref, south_ref, north_ref, last):
    lat = lax.axis_index("lat")
    even = lax.rem(lat, 2) == 0
    for start in range(0, MSG_ROWS, 8):
        a = recv_a_ref[pl.ds(start, 8), :]
        b = recv_b_ref[pl.ds(start, 8), :]
        south_ref[pl.ds(start, 8), :] = jnp.where(lat == 0, 0.0, jnp.where(even, b, a))
        north_ref[pl.ds(start, 8), :] = jnp.where(lat == last, 0.0, jnp.where(even, a, b))


def pack_interior_kernel(
    c_ref, adj_ref, zon_ref, mer_ref, depth_ref, diag_ref, o_ref, own_ref, late_ref, m_ref, f_ref, factor_ref
):
    lane = lane_iota()
    for level in range(16):
        factor_ref[level] = jnp.full((8, LANES), c_ref[level // 8, level % 8], jnp.float32)
    for tracer in range(2):
        by_group = jnp.zeros((8, LANES), jnp.float32)
        for k in range(8):
            by_group = jnp.where(lane // 16 == k, c_ref[tracer, k], by_group)
        factor_ref[16 + tracer] = by_group

    def rows(r, carry):
        at = aligned(8 * r)
        to = aligned(8 * r + HALO)
        depth = depth_ref[at, :].astype(jnp.float32)
        diag = diag_ref[at, :]
        masked = [jnp.where(depth > float(level % 8), adj_ref[level, at, :], 0.0) for level in range(16)]
        flows = [
            0.5 * ref[1, k, at, :].astype(jnp.float32) for ref in (zon_ref, mer_ref) for k in range(8)
        ]
        for level in range(16):
            m_ref[level, aligned(8 * r + 2 * HALO), :] = masked[level]
            f_ref[level, aligned(8 * r + 2 * HALO), :] = flows[level]
        o_ref[to, :] = pack_messages(masked, lane)
        o_ref[aligned(EXT + 8 * r + HALO), :] = pack_messages(flows, lane)
        o_ref[aligned(2 * EXT + 8 * r + HALO), :] = pack_surface(depth, diag, lane)
        own_ref[M0, to, :] = pack_own(masked[:8], lane)
        own_ref[M1, to, :] = pack_own(masked[8:], lane)
        own_ref[FU, to, :] = pack_own(flows[:8], lane)
        own_ref[FV, to, :] = pack_own(flows[8:], lane)
        own_ref[PDEP, to, :] = in_every_group(roll(depth, 8), lane)
        own_ref[PDIA, to, :] = in_every_group(roll(diag, 8), lane)
        for which, ref in enumerate((zon_ref, mer_ref)):
            late_ref[which, at, :] = pack_own([0.5 * ref[0, k, at, :].astype(jnp.float32) for k in range(8)], lane)
        return carry

    lax.fori_loop(0, ROWS // 8, rows, 0)


def make_pack_edges_kernel(last):
    def kernel(ra_ref, rb_ref, o_in_ref, o_ref, south_ref, north_ref):
        del o_in_ref
        sort_rows(ra_ref, rb_ref, south_ref, north_ref, last)
        lane = lane_iota()
        for ref, south, base in ((south_ref, True, 0), (north_ref, False, HALO + ROWS)):
            masked = [level_rows(ref, MASK_AT, 4, level, south) for level in range(16)]
            o_ref[base : base + 8, :] = pack_messages(masked, lane)
            flows = [level_rows(ref, FLOW_AT, 2, level, south) for level in range(16)]
            o_ref[EXT + base : EXT + base + 8, :] = pack_messages(flows, lane)
            depth = level_rows(ref, DEPTH_AT, 4, 0, south)
            diag = level_rows(ref, DIAG_AT, 4, 0, south)
            o_ref[2 * EXT + base : 2 * EXT + base + 8, :] = pack_surface(depth, diag, lane)

    return kernel


def rows_at(r, shift=0):
    start = HALO + 8 * r
    return pl.ds(pl.multiple_of(start, 8) if shift == 0 else start + shift, 8)


def star(ref, r):
    centre = ref[rows_at(r), :]
    return centre, roll(centre, 1), roll(centre, -1), ref[rows_at(r, -1), :], ref[rows_at(r, 1), :]


def shifted(ref, diag_ref, r):
    centre, west, east, south, north = star(ref, r)
    return diag_ref[rows_at(r), :] * centre - (west + east + south + north)


def on_grid(r, last, value):
    lat = lax.axis_index("lat")
    at = 8 * r + lax.broadcasted_iota(jnp.int32, (8, LANES), 0) - HALO
    beyond = ((at < 0) & (lat == 0)) | ((at >= ROWS) & (lat == last))
    return jnp.where(beyond, 0.0, value)


def apply(coef, centre, west, east, south, north):
    c0, cw, ce, cs, cn = coef
    return (c0 * centre + cw * west) + (ce * east + cs * south) + cn * north


def coefficients(u, w, mins, k):
    dep, dw, de, ds, dn = mins
    cw = jnp.where(dw > k, DIFF - u, 0.0)
    ce = jnp.where(de > k, DIFF + u, 0.0)
    cs = jnp.where(ds > k, DIFF - w, 0.0)
    cn = jnp.where(dn > k, DIFF + w, 0.0)
    c0 = jnp.where(dep > k, 1.0 - ((cw + ce) + (cs + cn)), 0.0)
    return c0, cw, ce, cs, cn


def depths(ref, r):
    dep, *others = star(ref, r)
    return [dep] + [jnp.minimum(dep, d) for d in others]


def products(b, h, hh, fields, image, second):
    new = [b * b, b * h, h * h, h * hh, b * hh]
    for left, right in ((fields, fields), (fields, image), (image, image), (image, second), (fields, second)):
        for i, j in PAIRS:
            if i == j or left is right:
                new.append(left[i] * right[j])
            else:
                new.append(left[i] * right[j] + left[j] * right[i])
    return new


def make_block_kernel(last):
    def kernel(
        c_ref, depth_ref, diag_ref, ra_ref, rb_ref, own_in_ref, m_in_ref, f_in_ref,
        am_ref, pq_ref, s_ref, sums_ref, shift_ref, own_ref, m_ref, f_ref,
        south_ref, north_ref,
    ):
        del own_in_ref, m_in_ref, f_in_ref
        lane = lane_iota()
        coup = [c_ref[level] for level in range(16)]
        square = [coup[k] * coup[k] + coup[k + 8] * coup[k + 8] for k in range(8)]
        sort_rows(ra_ref, rb_ref, south_ref, north_ref, last)
        lo, hi, mid = HALO, EXT, 2 * HALO
        for level in range(16):
            for ref, at, count in ((m_ref, MASK_AT, 4), (f_ref, FLOW_AT, 2)):
                ref[level, lo : lo + 8, :] = level_rows(south_ref, at, count, level, True)
                ref[level, hi : hi + 8, :] = level_rows(north_ref, at, count, level, False)
        for field, at in ((DEP, DEPTH_AT), (DIA, DIAG_AT)):
            s_ref[field, lo : lo + 8, :] = level_rows(south_ref, at, 4, 0, True)
            s_ref[field, hi : hi + 8, :] = level_rows(north_ref, at, 4, 0, False)

        s_ref[DEP, mid : mid + ROWS, :] = depth_ref[...].astype(jnp.float32)
        s_ref[DIA, mid : mid + ROWS, :] = diag_ref[...]

        def rhs(r, carry):
            at = rows_at(r)
            parts = [coup[level] * m_ref[level, at, :] for level in range(16)]
            while len(parts) > 1:
                parts = [parts[i] + parts[i + 1] for i in range(0, len(parts), 2)]
            s_ref[B, at, :] = parts[0]
            return carry

        lax.fori_loop(0, CHUNKS, rhs, 0)

        zero = jnp.zeros((8, LANES), jnp.float32)

        def quotient(r, carry):
            b = s_ref[B, rows_at(r), :]
            return carry[0] + b * b, carry[1] + b * shifted(s_ref.at[B], s_ref.at[DIA], r)

        squares, images_sum = lax.fori_loop(1, CHUNKS - 1, quotient, (zero, zero), unroll=2)
        inside = (lane > 0) & (lane < LANES - 1)
        squares, images_sum = [
            jnp.sum(jnp.sum(jnp.where(inside, v, 0.0), axis=0, keepdims=True), axis=1, keepdims=True)
            for v in (squares, images_sum)
        ]
        shift = jnp.where(squares > 0.0, images_sum / jnp.where(squares > 0.0, squares, 1.0), 0.0)
        shift = jnp.broadcast_to(jnp.clip(shift, -4.0, 5.0), (8, LANES))
        shift_ref[...] = shift

        def images(r, carry):
            s_ref[DIA, rows_at(r), :] = s_ref[DIA, rows_at(r), :] - shift
            s_ref[H, rows_at(r), :] = on_grid(r, last, shifted(s_ref.at[B], s_ref.at[DIA], r))
            return carry

        lax.fori_loop(0, CHUNKS, images, 0, unroll=2)

        def advect(r, carry):
            out_at = aligned(8 * r)
            at, below, above = rows_at(r), rows_at(r, -1), rows_at(r, 1)
            mins = depths(s_ref.at[DEP], r)
            bs = star(s_ref.at[B], r)
            hs = star(s_ref.at[H], r)
            us = vs = ws = jnp.zeros((8, LANES), jnp.float32)
            for k in range(8):
                coef = coefficients(f_ref[k, at, :], f_ref[8 + k, at, :], mins, float(k))
                for level in (k, k + 8):
                    centre = m_ref[level, at, :]
                    value = apply(
                        coef, centre, roll(centre, 1), roll(centre, -1),
                        m_ref[level, below, :], m_ref[level, above, :],
                    )
                    am_ref[level, out_at, :] = value
                    us = us + coup[level] * value
                p = apply(coef, *bs)
                q = apply(coef, *hs)
                pq_ref[k, out_at, :] = p
                pq_ref[8 + k, out_at, :] = q
                vs = vs + square[k] * p
                ws = ws + square[k] * q
            s_ref[U, at, :] = us
            s_ref[V, at, :] = vs
            s_ref[W, at, :] = ws
            return carry

        lax.fori_loop(0, CHUNKS, advect, 0)

        def images_two(r, carry):
            for source, target in ((U, HU), (V, HV), (W, HW)):
                s_ref[target, rows_at(r), :] = on_grid(r, last, shifted(s_ref.at[source], s_ref.at[DIA], r))
            return carry

        lax.fori_loop(0, CHUNKS, images_two, 0, unroll=2)

        def gather(r, sums):
            at = rows_at(r)
            hh, *second = [shifted(s_ref.at[field], s_ref.at[DIA], r) for field in (H, HU, HV, HW)]
            b, h, *rest = [s_ref[field, at, :] for field in (B, H, U, V, W, HU, HV, HW)]
            return tuple(s + n for s, n in zip(sums, products(b, h, hh, rest[:3], rest[3:], second)))

        sums = lax.fori_loop(1, CHUNKS - 1, gather, (zero,) * NSUMS)
        keep = (lane >= FIRST) & (lane <= LAST)
        for index, value in enumerate(sums):
            sums_ref[8 * index : 8 * index + 8, :] = jnp.where(keep, value, 0.0)

        for ref, south, base in ((south_ref, True, 0), (north_ref, False, HALO + ROWS)):
            rows = pl.ds(base, 8)
            for slot, at, count in ((M0, MASK_AT, 4), (FU, FLOW_AT, 2)):
                values = [level_rows(ref, at, count, level, south) for level in range(16)]
                own_ref[slot, rows, :] = pack_own(values[:8], lane)
                own_ref[slot + 1, rows, :] = pack_own(values[8:], lane)
            for slot, at in ((PDEP, DEPTH_AT), (PDIA, DIAG_AT)):
                own_ref[slot, rows, :] = in_every_group(roll(level_rows(ref, at, 4, 0, south), 8), lane)

    return kernel


def make_sides_kernel(last, devices):
    def kernel(
        c_ref, own_ref, pb_ref, pa_ref, block_sums_ref, shift_ref, z_ref, s_ref, sums_ref, m_ref, f_ref, all_ref
    ):
        lane = lane_iota()
        pos = lane % 16
        level_of = (lane // 16).astype(jnp.float32)
        first, second = c_ref[16], c_ref[17]
        square = first * first + second * second
        even_lon = lax.rem(lax.axis_index("lon"), 2) == 0
        shift = shift_ref[...]

        def assemble(r, carry):
            at = rows_at(r)
            own_at = aligned(8 * r)
            for side in range(2):
                outer = pos >= 8 if side == 0 else pos < 8
                for part in range(3):
                    src = aligned(part * EXT + 8 * r)
                    a, b = pa_ref[src, :], pb_ref[src, :]
                    got = jnp.where(even_lon, a, b) if side == 0 else jnp.where(even_lon, b, a)
                    one = jnp.where(outer, roll(got, 4), own_ref[2 * part, own_at, :])
                    two = jnp.where(outer, roll(got, -4), own_ref[2 * part + 1, own_at, :])
                    if part == 0:
                        m_ref[side, 0, at, :] = one
                        m_ref[side, 1, at, :] = two
                        s_ref[side, B, at, :] = over_groups(first * one + second * two)
                    elif part == 1:
                        f_ref[side, 0, at, :] = one
                        f_ref[side, 1, at, :] = two
                    else:
                        s_ref[side, DEP, at, :] = one
                        s_ref[side, DIA, at, :] = two - shift
            return carry

        lax.fori_loop(0, CHUNKS, assemble, 0, unroll=10)

        def images(r, carry):
            for side in range(2):
                value = shifted(s_ref.at[side, B], s_ref.at[side, DIA], r)
                s_ref[side, H, rows_at(r), :] = on_grid(r, last, value)
            return carry

        lax.fori_loop(0, CHUNKS, images, 0, unroll=10)

        def advect(r, carry):
            at, out_at = rows_at(r), aligned(8 * r)
            for side in range(2):
                mins = depths(s_ref.at[side, DEP], r)
                coef = coefficients(f_ref[side, 0, at, :], f_ref[side, 1, at, :], mins, level_of)
                one = apply(coef, *star(m_ref.at[side, 0], r))
                two = apply(coef, *star(m_ref.at[side, 1], r))
                p = apply(coef, *star(s_ref.at[side, B], r))
                q = apply(coef, *star(s_ref.at[side, H], r))
                for slot, value in enumerate((one, two, p, q)):
                    z_ref[side, slot, out_at, :] = value
                s_ref[side, U, at, :] = over_groups(first * one + second * two)
                s_ref[side, V, at, :] = over_groups(square * p)
                s_ref[side, W, at, :] = over_groups(square * q)
            return carry

        lax.fori_loop(0, CHUNKS, advect, 0, unroll=5)

        def images_two(r, carry):
            for side in range(2):
                for source, target in ((U, HU), (V, HV), (W, HW)):
                    value = shifted(s_ref.at[side, source], s_ref.at[side, DIA], r)
                    s_ref[side, target, rows_at(r), :] = on_grid(r, last, value)
            return carry

        lax.fori_loop(0, CHUNKS, images_two, 0, unroll=5)

        east = lane < 8

        def gather(r, sums):
            at = rows_at(r)

            def both(field):
                return jnp.where(east, s_ref[0, field, at, :], s_ref[1, field, at, :])

            def image(field):
                one, two = [shifted(s_ref.at[side, field], s_ref.at[side, DIA], r) for side in range(2)]
                return jnp.where(east, one, two)

            hh, *second_image = [image(field) for field in (H, HU, HV, HW)]
            b, h, *rest = [both(field) for field in (B, H, U, V, W, HU, HV, HW)]
            return tuple(s + n for s, n in zip(sums, products(b, h, hh, rest[:3], rest[3:], second_image)))

        zero = jnp.zeros((8, LANES), jnp.float32)
        sums = lax.fori_loop(1, CHUNKS - 1, gather, (zero,) * NSUMS, unroll=1)
        keep = (lane >= 4) & (lane < 12)
        for index, value in enumerate(sums):
            at = pl.ds(8 * index, 8)
            all_ref[at, :] = block_sums_ref[at, :] + jnp.where(keep, value, 0.0)
        for index in range(NSUMS, SUM_ROWS):
            all_ref[pl.ds(8 * index, 8), :] = zero
        row = lax.broadcasted_iota(jnp.int32, (8, LANES), 0)
        line = jnp.zeros((8, LANES), jnp.float32)
        for base in range(0, SUM_ROWS, 8):
            total = all_ref[pl.ds(8 * base, 8, stride=8), :]
            for sub in range(1, 8):
                total = total + all_ref[pl.ds(8 * base + sub, 8, stride=8), :]
            total = jnp.sum(total, axis=1, keepdims=True)
            line = jnp.where(lane == base + row, total, line)
        line = jnp.sum(line, axis=0, keepdims=True)
        line = jnp.where(lane[0:1, :] == NSUMS, shift[0:1, :], line)
        sums_ref[...] = jnp.broadcast_to(line, (devices, LANES))

    return kernel


def solve(m0, m1, m2, m3, m4, shift):
    def over_devices(x):
        return jnp.sum(x, axis=1, keepdims=True)

    norm = over_devices(m0)
    mean = over_devices(m1 + shift * m0) / norm
    theta = mean + SHIFT
    delta = shift - mean
    spread = over_devices(m2 + delta * (2.0 * m1 + delta * m0))
    curve = over_devices(m3 + delta * (2.0 * m2 + m4 + delta * (3.0 * m1 + delta * m0)))
    ratio = spread / (theta * theta * norm)
    gamma = curve / spread + theta * (1.0 - ratio)
    image = -1.0 / (theta * gamma)
    return 1.0 / theta + ratio / gamma + delta * image, image


def make_finish_kernel(lat_count):
    def kernel(
        c_ref, zon_ref, mer_ref, am_ref, pq_ref, s_ref, late_ref, z_ref, side_ref, sums_ref,
        out_ref, sens_ref, m_ref, zm_ref, zx_ref,
    ):
        lane = lane_iota()
        pos = lane % 16
        level_of = (lane // 16).astype(jnp.float32)
        coup = [c_ref[level] for level in range(16)]
        first, second = c_ref[16], c_ref[17]

        devices = sums_ref.shape[0]
        blocks = []
        for base in range(0, devices, LANES):
            part = sums_ref[base : min(base + LANES, devices), :]
            if part.shape[0] < LANES:
                part = jnp.concatenate([part, jnp.zeros((LANES - part.shape[0], LANES), jnp.float32)], axis=0)
            blocks.append(jnp.transpose(part))
        turned = blocks[0] if len(blocks) == 1 else jnp.concatenate(blocks, axis=1)
        rows = [turned[i : i + 1, :] for i in range(NSUMS + 1)]
        shift = rows[NSUMS]
        near, e1 = solve(*rows[:5], shift)
        factor = (None, near, e1, near * near, near * e1, e1 * e1)
        moments = []
        for kind in range(5):
            base = 5 + kind * len(PAIRS)
            value = rows[base]
            for index in range(1, len(PAIRS)):
                twice = 2.0 if kind in (0, 2) and index in (1, 2, 4) else 1.0
                value = value + (twice * factor[index]) * rows[base + index]
            moments.append(value)
        late, e0 = solve(*moments, shift)
        me = lax.axis_index("lon") * lat_count + lax.axis_index("lat")
        mine = lax.broadcasted_iota(jnp.int32, shift.shape, 1) == me
        a1, a0 = [jnp.sum(jnp.where(mine, v, 0.0), axis=1, keepdims=True) for v in (near, late)]
        a1, e1, a0, e0 = [jnp.broadcast_to(v, (8, LANES)) for v in (a1, e1, a0, e0)]

        def surface(ref, at):
            b = ref[U, at, :] + a1 * ref[V, at, :] + e1 * ref[W, at, :]
            h = ref[HU, at, :] + a1 * ref[HV, at, :] + e1 * ref[HW, at, :]
            x = a0 * b + e0 * h
            return x, x + (a1 * ref[B, at, :] + e1 * ref[H, at, :])

        def middle(r, carry):
            at, to = aligned(8 * r), rows_at(r)
            for side in range(2):
                x, both_steps = surface(side_ref.at[side], to)
                zx_ref[side, at, :] = both_steps
                part = a1 * z_ref[side, 2, at, :] + e1 * z_ref[side, 3, at, :]
                part = part + jnp.where(side_ref[side, DEP, to, :] > level_of, x, 0.0)
                zm_ref[side, 0, to, :] = z_ref[side, 0, at, :] + first * part
                zm_ref[side, 1, to, :] = z_ref[side, 1, at, :] + second * part
            x, both_steps = surface(s_ref, to)
            zx_ref[2, at, :] = both_steps
            dep = s_ref[DEP, to, :]
            for k in range(8):
                part = a1 * pq_ref[k, at, :] + e1 * pq_ref[8 + k, at, :] + jnp.where(dep > float(k), x, 0.0)
                for level in (k, k + 8):
                    m_ref[level, to, :] = am_ref[level, at, :] + coup[level] * part
            return carry

        lax.fori_loop(0, CHUNKS, middle, 0, unroll=2)

        edge = (lane < FIRST) | (lane > LAST)

        def advect(i, carry):
            r = i + 1
            out_at = aligned(8 * i)
            ext_at = aligned(8 * r)
            at, below, above = rows_at(r), rows_at(r, -1), rows_at(r, 1)
            sides = []
            for side in range(2):
                mins = depths(side_ref.at[side, DEP], r)
                coef = coefficients(late_ref[0, out_at, :], late_ref[1, out_at, :], mins, level_of)
                sides.append([apply(coef, *star(zm_ref.at[side, t], r)) for t in range(2)])
            inserts = [jnp.where(pos < 8, sides[0][t], sides[1][t]) for t in range(2)]
            ins = jnp.where(pos < 8, zx_ref[0, ext_at, :], zx_ref[1, ext_at, :])
            sens_ref[out_at, :] = jnp.where(edge, roll(ins, -8), zx_ref[2, ext_at, :])
            mins = depths(s_ref.at[DEP], r)
            for k in range(8):
                u = 0.5 * zon_ref[0, k, out_at, :].astype(jnp.float32)
                w = 0.5 * mer_ref[0, k, out_at, :].astype(jnp.float32)
                coef = coefficients(u, w, mins, float(k))
                for level in (k, k + 8):
                    centre = m_ref[level, at, :]
                    value = apply(
                        coef, centre, roll(centre, 1), roll(centre, -1),
                        m_ref[level, below, :], m_ref[level, above, :],
                    )
                    value = jnp.where(edge, roll(inserts[level // 8], -own_shift(k)), value)
                    out_ref[level, out_at, :] = value
            return carry

        lax.fori_loop(0, ROWS // 8, advect, 0, unroll=2)

    return kernel


VMEM = pl.BlockSpec(memory_space=pltpu.VMEM)
HBM = pl.BlockSpec(memory_space=pltpu.HBM)


def on_device_of(lon, lat):
    devices = lon * lat
    f32 = jnp.float32

    def array(*shape):
        return jax.ShapeDtypeStruct(shape, f32)

    smem = pl.BlockSpec(memory_space=pltpu.SMEM)
    params = pltpu.CompilerParams(vmem_limit_bytes=48 * 2**20)
    pairs = {}
    for axis, count in (("lon", lon), ("lat", lat)):
        first = [(i, i ^ 1) for i in range(count)]
        second = [(i, (i - 1) % count if i % 2 == 0 else (i + 1) % count) for i in range(count)]
        pairs[axis] = (first, second)

    def swap(axis, a, b):
        first, second = pairs[axis]
        return lax.ppermute(a, axis, first), lax.ppermute(b, axis, second)

    def on_device(adj_tracer, zonal_flow, meridional_flow, depth, coupling, surface_diag):
        adj = adj_tracer.reshape(16, ROWS, LANES)
        block_args = (adj, zonal_flow, meridional_flow, depth, surface_diag)
        msg_a, msg_b = pl.pallas_call(
            row_message_kernel,
            in_specs=[HBM] * 5,
            out_specs=[VMEM] * 2,
            out_shape=[array(MSG_ROWS, LANES)] * 2,
            scratch_shapes=[
                pltpu.VMEM((2, 16, 8, LANES), f32),
                pltpu.VMEM((2, 2, 8, 8, LANES), jnp.bfloat16),
                pltpu.VMEM((2, 8, LANES), jnp.int32),
                pltpu.VMEM((2, 8, LANES), f32),
                pltpu.SemaphoreType.DMA((10,)),
            ],
            compiler_params=pltpu.CompilerParams(vmem_limit_bytes=62914560),
            name="row_messages",
        )(*block_args)
        recv_a, recv_b = swap("lat", msg_a, msg_b)
        packed, own, late, masked, flows, factors = pl.pallas_call(
            pack_interior_kernel,
            in_specs=[smem] + [VMEM] * 5,
            out_specs=[VMEM] * 6,
            out_shape=[
                array(3 * EXT, LANES), array(6, EXT, LANES), array(2, ROWS, LANES),
                array(16, PAD, LANES), array(16, PAD, LANES), array(18, 8, LANES),
            ],
            compiler_params=params,
            cost_estimate=pl.CostEstimate(flops=4_000_000, bytes_accessed=1_000_000, transcendentals=0),
            name="pack_interior",
        )(coupling, *block_args)
        row_scratch = [pltpu.VMEM((MSG_ROWS, LANES), f32)] * 2
        packed = pl.pallas_call(
            make_pack_edges_kernel(lat - 1),
            in_specs=[VMEM] * 3,
            out_specs=VMEM,
            out_shape=array(3 * EXT, LANES),
            scratch_shapes=row_scratch,
            input_output_aliases={2: 0},
            compiler_params=params,
            name="pack_edges",
        )(recv_a, recv_b, packed)
        side_a, side_b = swap("lon", packed, packed)
        am, pq, block, block_sums, shift, own, _, _ = pl.pallas_call(
            make_block_kernel(lat - 1),
            in_specs=[VMEM] * 8,
            out_specs=[VMEM] * 8,
            out_shape=[
                array(16, EXT, LANES), array(16, EXT, LANES), array(10, PAD, LANES),
                array(8 * NSUMS, LANES), array(8, LANES), array(6, EXT, LANES),
                array(16, PAD, LANES), array(16, PAD, LANES),
            ],
            scratch_shapes=row_scratch,
            input_output_aliases={5: 5, 6: 6, 7: 7},
            compiler_params=params,
            cost_estimate=pl.CostEstimate(flops=16_000_000, bytes_accessed=4_000_000, transcendentals=0),
            name="block",
        )(factors, depth, surface_diag, recv_a, recv_b, own, masked, flows)
        z, sides, sums = pl.pallas_call(
            make_sides_kernel(lat - 1, devices),
            in_specs=[VMEM] * 6,
            out_specs=[VMEM] * 3,
            out_shape=[array(2, 4, EXT, LANES), array(2, 10, PAD, LANES), array(devices, LANES)],
            scratch_shapes=[
                pltpu.VMEM((2, 2, PAD, LANES), f32),
                pltpu.VMEM((2, 2, PAD, LANES), f32),
                pltpu.VMEM((8 * SUM_ROWS, LANES), f32),
            ],
            compiler_params=params,
            name="sides",
        )(factors, own, side_b, side_a, block_sums, shift)
        everyone = lax.all_to_all(sums, ("lon", "lat"), 0, 0, tiled=True)
        out, sens = pl.pallas_call(
            make_finish_kernel(lat),
            in_specs=[VMEM] * 10,
            out_specs=[VMEM] * 2,
            out_shape=[array(16, ROWS, LANES), array(ROWS, LANES)],
            scratch_shapes=[
                pltpu.VMEM((16, PAD, LANES), f32),
                pltpu.VMEM((2, 2, PAD, LANES), f32),
                pltpu.VMEM((3, EXT, LANES), f32),
            ],
            compiler_params=params,
            name="finish",
        )(factors, zonal_flow, meridional_flow, am, pq, block, late, z, sides, everyone)
        return out.reshape(adj_tracer.shape), sens

    return on_device


def solution(mesh):
    in_specs = (
        P(None, None, "lat", "lon"),
        P(None, None, "lat", "lon"),
        P(None, None, "lat", "lon"),
        P("lat", "lon"),
        P(),
        P("lat", "lon"),
    )
    out_specs = (P(None, None, "lat", "lon"), P("lat", "lon"))
    return jax.shard_map(
        on_device_of(mesh.shape["lon"], mesh.shape["lat"]),
        mesh=mesh, in_specs=in_specs, out_specs=out_specs, check_vma=False,
    )
```

```python
import jax
import jax.numpy as jnp
from jax import lax
from jax.experimental import pallas as pl
from jax.experimental.pallas import tpu as pltpu
from jax.sharding import PartitionSpec as P

DIFF = 0.15
SHIFT = 4.0
LANES = 128
ROWS = 64
HALO = 8
EXT = ROWS + 2 * HALO
PAD = EXT + 2 * HALO
CHUNKS = EXT // 8
FLOW_AT, MASK_AT, DEPTH_AT, DIAG_AT, MSG_ROWS = 8, 40, 104, 108, 120
DEP, DIA, B, H, U, V, W, HU, HV, HW = range(10)
M0, M1, FU, FV, PDEP, PDIA = range(6)
SIDE_ROWS = EXT + 8
FIRST, LAST = 4, LANES - 5
PAIRS = ((0, 0), (0, 1), (0, 2), (1, 1), (1, 2), (2, 2))
NSUMS = 5 + 5 * len(PAIRS)
SUM_ROWS = 40


def lane_iota():
    return lax.broadcasted_iota(jnp.int32, (8, LANES), 1)


def roll(x, by):
    by = by % LANES
    return pltpu.roll(x, by, 1) if by else x


def over_groups(x):
    for by in (16, 32, 64):
        x = x + roll(x, by)
    return x


def in_every_group(x, lane):
    return over_groups(jnp.where(lane < 16, x, 0.0))


def own_shift(level):
    return 16 * (level % 8) + 8


def pack_own(values, lane):
    packed = roll(values[0], own_shift(0))
    for level in range(1, 8):
        packed = jnp.where(lane // 16 == level, roll(values[level], own_shift(level)), packed)
    return packed


def side_messages(own, surface, lane):
    pos = lane % 16
    third = pos // 4

    def merge(parts):
        value = parts[0]
        for index in range(1, 4):
            value = jnp.where(third == index, parts[index], value)
        return value

    to_east = merge([roll(own[0], -4), own[1], roll(own[2], 4), roll(own[3], 8)])
    to_west = merge([roll(own[0], -8), roll(own[1], -4), own[2], roll(own[3], 4)])
    depth, diag = surface
    east = jnp.where(pos < 4, roll(depth, -4), diag)
    west = jnp.where(pos < 4, roll(depth, -8), roll(diag, -4))
    east, west = [jnp.where(pos < 8, v, roll(v, 8)) for v in (east, west)]
    return to_east, to_west, east, west


def aligned(start, count=8):
    return pl.ds(pl.multiple_of(start, 8), count)


def level_rows(ref, at, count, index, south):
    start = at + count * index
    return ref[pl.ds(start - (8 - count) if south else start, 8), :]


def row_message_kernel(adj, zon, mer, depth, diag, a_ref, b_ref, adj_ref, flow_ref, depth_ref, diag_ref, sems):
    copies = []
    for edge, start in ((0, 0), (1, ROWS - 8)):
        rows = pl.ds(start, 8)
        for source, target in (
            (adj.at[:, rows, :], adj_ref.at[edge]),
            (zon.at[1, :, rows, :], flow_ref.at[edge, 0]),
            (mer.at[1, :, rows, :], flow_ref.at[edge, 1]),
            (depth.at[rows, :], depth_ref.at[edge]),
            (diag.at[rows, :], diag_ref.at[edge]),
        ):
            copies.append(pltpu.make_async_copy(source, target, sems.at[len(copies)]))
            copies[-1].start()
    even = lax.rem(lax.axis_index("lat"), 2) == 0
    zero = jnp.zeros((8, LANES), jnp.float32)
    for ref in (a_ref, b_ref):
        ref[0:8, :] = zero
        ref[MSG_ROWS - 8 : MSG_ROWS, :] = zero
    for copy in copies:
        copy.wait()

    def put(at, low, high):
        count = low.shape[0]
        a_ref[pl.ds(at, count), :] = jnp.where(even, high, low)
        b_ref[pl.ds(at, count), :] = jnp.where(even, low, high)

    depth_low = depth_ref[0, 0:4, :].astype(jnp.float32)
    depth_high = depth_ref[1, 4:8, :].astype(jnp.float32)
    for level in range(16):
        k = float(level % 8)
        low = jnp.where(depth_low > k, adj_ref[0, level, 0:4, :], 0.0)
        high = jnp.where(depth_high > k, adj_ref[1, level, 4:8, :], 0.0)
        put(MASK_AT + 4 * level, low, high)
    put(DEPTH_AT, depth_low, depth_high)
    put(DIAG_AT, diag_ref[0, 0:4, :], diag_ref[1, 4:8, :])
    for level in range(16):
        low = 0.5 * flow_ref[0, level // 8, level % 8].astype(jnp.float32)
        high = 0.5 * flow_ref[1, level // 8, level % 8].astype(jnp.float32)
        put(FLOW_AT + 2 * level, low[0:2], high[6:8])


def sort_rows(recv_a_ref, recv_b_ref, south_ref, north_ref, last):
    lat = lax.axis_index("lat")
    even = lax.rem(lat, 2) == 0
    for start in range(0, MSG_ROWS, 8):
        a = recv_a_ref[pl.ds(start, 8), :]
        b = recv_b_ref[pl.ds(start, 8), :]
        south_ref[pl.ds(start, 8), :] = jnp.where(lat == 0, 0.0, jnp.where(even, b, a))
        north_ref[pl.ds(start, 8), :] = jnp.where(lat == last, 0.0, jnp.where(even, a, b))


def pack_interior_kernel(
    c_ref, adj_ref, zon_ref, mer_ref, depth_ref, diag_ref,
    a_ref, b_ref, own_ref, late_ref, m_ref, f_ref, s_ref, factor_ref,
):
    lane = lane_iota()
    even = lax.rem(lax.axis_index("lon"), 2) == 0
    coup = [jnp.full((8, LANES), c_ref[level // 8, level % 8], jnp.float32) for level in range(16)]
    for level in range(16):
        factor_ref[level] = coup[level]
    for tracer in range(2):
        by_group = jnp.zeros((8, LANES), jnp.float32)
        for k in range(8):
            by_group = jnp.where(lane // 16 == k, c_ref[tracer, k], by_group)
        factor_ref[16 + tracer] = by_group

    def rows(r, carry):
        at = aligned(8 * r)
        to = aligned(8 * r + HALO)
        far = aligned(8 * r + 2 * HALO)
        depth = depth_ref[at, :].astype(jnp.float32)
        diag = diag_ref[at, :]
        s_ref[DEP, far, :] = depth
        s_ref[DIA, far, :] = diag
        masked = [jnp.where(depth > float(level % 8), adj_ref[level, at, :], 0.0) for level in range(16)]
        flows = [
            0.5 * ref[1, k, at, :].astype(jnp.float32) for ref in (zon_ref, mer_ref) for k in range(8)
        ]
        for level in range(16):
            m_ref[level, far, :] = masked[level]
            f_ref[level, far, :] = flows[level]
        parts = [factor_ref[level] * masked[level] for level in range(16)]
        while len(parts) > 1:
            parts = [parts[i] + parts[i + 1] for i in range(0, len(parts), 2)]
        s_ref[B, far, :] = parts[0]
        own = [pack_own(v, lane) for v in (masked[:8], masked[8:], flows[:8], flows[8:])]
        surface = [in_every_group(roll(v, 8), lane) for v in (depth, diag)]
        for slot, value in enumerate(own + surface):
            own_ref[slot, to, :] = value
        to_east, to_west, east, west = side_messages(own, surface, lane)
        a_ref[to, :] = jnp.where(even, to_east, to_west)
        b_ref[to, :] = jnp.where(even, to_west, to_east)
        here = lane // 8 == r + 1
        for which, ref in enumerate((zon_ref, mer_ref)):
            late_ref[which, at, :] = pack_own([0.5 * ref[0, k, at, :].astype(jnp.float32) for k in range(8)], lane)
        return jnp.where(here, east, carry[0]), jnp.where(here, west, carry[1])

    zero = jnp.zeros((8, LANES), jnp.float32)
    east, west = lax.fori_loop(0, ROWS // 8, rows, (zero, zero), unroll=2)
    a_ref[EXT : EXT + 8, :] = jnp.where(even, east, west)
    b_ref[EXT : EXT + 8, :] = jnp.where(even, west, east)


def make_pack_edges_kernel(last):
    def kernel(ra_ref, rb_ref, a_in_ref, b_in_ref, own_in_ref, a_ref, b_ref, own_ref, south_ref, north_ref):
        del own_in_ref
        sort_rows(ra_ref, rb_ref, south_ref, north_ref, last)
        lane = lane_iota()
        even = lax.rem(lax.axis_index("lon"), 2) == 0
        surface_a, surface_b = [ref[EXT : EXT + 8, :] for ref in (a_in_ref, b_in_ref)]
        for ref, south, base in ((south_ref, True, 0), (north_ref, False, HALO + ROWS)):
            rows = pl.ds(base, 8)
            masked = [level_rows(ref, MASK_AT, 4, level, south) for level in range(16)]
            flows = [level_rows(ref, FLOW_AT, 2, level, south) for level in range(16)]
            own = [pack_own(v, lane) for v in (masked[:8], masked[8:], flows[:8], flows[8:])]
            surface = [in_every_group(roll(level_rows(ref, at, 4, 0, south), 8), lane) for at in (DEPTH_AT, DIAG_AT)]
            for slot, value in enumerate(own + surface):
                own_ref[slot, rows, :] = value
            to_east, to_west, east, west = side_messages(own, surface, lane)
            a_ref[rows, :] = jnp.where(even, to_east, to_west)
            b_ref[rows, :] = jnp.where(even, to_west, to_east)
            here = lane // 8 == base // 8
            surface_a = jnp.where(here, jnp.where(even, east, west), surface_a)
            surface_b = jnp.where(here, jnp.where(even, west, east), surface_b)
        a_ref[EXT : EXT + 8, :] = surface_a
        b_ref[EXT : EXT + 8, :] = surface_b

    return kernel


def rows_at(r, shift=0):
    start = HALO + 8 * r
    return pl.ds(pl.multiple_of(start, 8) if shift == 0 else start + shift, 8)


def star(ref, r):
    centre = ref[rows_at(r), :]
    return centre, roll(centre, 1), roll(centre, -1), ref[rows_at(r, -1), :], ref[rows_at(r, 1), :]


def shifted(ref, diag_ref, r):
    centre, west, east, south, north = star(ref, r)
    return diag_ref[rows_at(r), :] * centre - (west + east + south + north)


def on_grid(r, last, value):
    lat = lax.axis_index("lat")
    at = 8 * r + lax.broadcasted_iota(jnp.int32, (8, LANES), 0) - HALO
    beyond = ((at < 0) & (lat == 0)) | ((at >= ROWS) & (lat == last))
    return jnp.where(beyond, 0.0, value)


def apply(coef, centre, west, east, south, north):
    c0, cw, ce, cs, cn = coef
    return (c0 * centre + cw * west) + (ce * east + cs * south) + cn * north


def coefficients(u, w, mins, k):
    dep, dw, de, ds, dn = mins
    cw = jnp.where(dw > k, DIFF - u, 0.0)
    ce = jnp.where(de > k, DIFF + u, 0.0)
    cs = jnp.where(ds > k, DIFF - w, 0.0)
    cn = jnp.where(dn > k, DIFF + w, 0.0)
    c0 = jnp.where(dep > k, 1.0 - ((cw + ce) + (cs + cn)), 0.0)
    return c0, cw, ce, cs, cn


def depths(ref, r):
    dep, *others = star(ref, r)
    return [dep] + [jnp.minimum(dep, d) for d in others]


def products(b, h, hh, fields, image, second):
    new = [b * b, b * h, h * h, h * hh, b * hh]
    for left, right in ((fields, fields), (fields, image), (image, image), (image, second), (fields, second)):
        for i, j in PAIRS:
            if i == j or left is right:
                new.append(left[i] * right[j])
            else:
                new.append(left[i] * right[j] + left[j] * right[i])
    return new


def make_block_kernel(last):
    def kernel(
        c_ref, ra_ref, rb_ref, m_in_ref, f_in_ref, s_in_ref,
        am_ref, pq_ref, sums_ref, shift_ref, m_ref, f_ref, s_ref,
        south_ref, north_ref,
    ):
        del m_in_ref, f_in_ref, s_in_ref
        lane = lane_iota()
        coup = [c_ref[level] for level in range(16)]
        square = [coup[k] * coup[k] + coup[k + 8] * coup[k + 8] for k in range(8)]
        sort_rows(ra_ref, rb_ref, south_ref, north_ref, last)
        lo, hi = HALO, EXT
        for level in range(16):
            for ref, at, count in ((m_ref, MASK_AT, 4), (f_ref, FLOW_AT, 2)):
                ref[level, lo : lo + 8, :] = level_rows(south_ref, at, count, level, True)
                ref[level, hi : hi + 8, :] = level_rows(north_ref, at, count, level, False)
        for field, at in ((DEP, DEPTH_AT), (DIA, DIAG_AT)):
            s_ref[field, lo : lo + 8, :] = level_rows(south_ref, at, 4, 0, True)
            s_ref[field, hi : hi + 8, :] = level_rows(north_ref, at, 4, 0, False)

        for r in (0, CHUNKS - 1):
            at = rows_at(r)
            parts = [coup[level] * m_ref[level, at, :] for level in range(16)]
            while len(parts) > 1:
                parts = [parts[i] + parts[i + 1] for i in range(0, len(parts), 2)]
            s_ref[B, at, :] = parts[0]

        zero = jnp.zeros((8, LANES), jnp.float32)

        def quotient(r, carry):
            b = s_ref[B, rows_at(r), :]
            return carry[0] + b * b, carry[1] + b * shifted(s_ref.at[B], s_ref.at[DIA], r)

        squares, images_sum = lax.fori_loop(1, CHUNKS - 1, quotient, (zero, zero), unroll=8)
        inside = (lane > 0) & (lane < LANES - 1)
        squares, images_sum = [
            jnp.sum(jnp.sum(jnp.where(inside, v, 0.0), axis=0, keepdims=True), axis=1, keepdims=True)
            for v in (squares, images_sum)
        ]
        shift = jnp.where(squares > 0.0, images_sum / jnp.where(squares > 0.0, squares, 1.0), 0.0)
        shift = jnp.broadcast_to(jnp.clip(shift, -4.0, 5.0), (8, LANES))
        shift_ref[...] = shift

        def images(r, carry):
            s_ref[DIA, rows_at(r), :] = s_ref[DIA, rows_at(r), :] - shift
            s_ref[H, rows_at(r), :] = on_grid(r, last, shifted(s_ref.at[B], s_ref.at[DIA], r))
            return carry

        lax.fori_loop(0, CHUNKS, images, 0, unroll=10)

        def advect(r, carry):
            out_at = aligned(8 * r)
            at, below, above = rows_at(r), rows_at(r, -1), rows_at(r, 1)
            mins = depths(s_ref.at[DEP], r)
            bs = star(s_ref.at[B], r)
            hs = star(s_ref.at[H], r)
            us = vs = ws = jnp.zeros((8, LANES), jnp.float32)
            for k in range(8):
                coef = coefficients(f_ref[k, at, :], f_ref[8 + k, at, :], mins, float(k))
                for level in (k, k + 8):
                    centre = m_ref[level, at, :]
                    value = apply(
                        coef, centre, roll(centre, 1), roll(centre, -1),
                        m_ref[level, below, :], m_ref[level, above, :],
                    )
                    am_ref[level, out_at, :] = value
                    us = us + coup[level] * value
                p = apply(coef, *bs)
                q = apply(coef, *hs)
                pq_ref[k, out_at, :] = p
                pq_ref[8 + k, out_at, :] = q
                vs = vs + square[k] * p
                ws = ws + square[k] * q
            s_ref[U, at, :] = us
            s_ref[V, at, :] = vs
            s_ref[W, at, :] = ws
            return carry

        lax.fori_loop(0, CHUNKS, advect, 0)

        def images_two(r, carry):
            for source, target in ((U, HU), (V, HV), (W, HW)):
                s_ref[target, rows_at(r), :] = on_grid(r, last, shifted(s_ref.at[source], s_ref.at[DIA], r))
            return carry

        lax.fori_loop(0, CHUNKS, images_two, 0, unroll=5)

        def gather(r, sums):
            at = rows_at(r)
            hh, *second = [shifted(s_ref.at[field], s_ref.at[DIA], r) for field in (H, HU, HV, HW)]
            b, h, *rest = [s_ref[field, at, :] for field in (B, H, U, V, W, HU, HV, HW)]
            return tuple(s + n for s, n in zip(sums, products(b, h, hh, rest[:3], rest[3:], second)))

        sums = lax.fori_loop(1, CHUNKS - 1, gather, (zero,) * NSUMS, unroll=2)
        keep = (lane >= FIRST) & (lane <= LAST)
        for index, value in enumerate(sums):
            sums_ref[8 * index : 8 * index + 8, :] = jnp.where(keep, value, 0.0)

    return kernel


def make_sides_kernel(last, devices):
    def kernel(
        c_ref, own_ref, pb_ref, pa_ref, block_sums_ref, shift_ref, z_ref, s_ref, sums_ref, m_ref, f_ref, all_ref
    ):
        lane = lane_iota()
        pos = lane % 16
        level_of = (lane // 16).astype(jnp.float32)
        first, second = c_ref[16], c_ref[17]
        square = first * first + second * second
        even_lon = lax.rem(lax.axis_index("lon"), 2) == 0
        shift = shift_ref[...]

        a_last, b_last = pa_ref[EXT : EXT + 8, :], pb_ref[EXT : EXT + 8, :]
        surfaces = (jnp.where(even_lon, a_last, b_last), jnp.where(even_lon, b_last, a_last))

        def assemble(r):
            at, rows = pl.ds(8 * r + HALO, 8), pl.ds(8 * r, 8)
            for side in range(2):
                outer = pos >= 8 if side == 0 else pos < 8
                a, b = pa_ref[rows, :], pb_ref[rows, :]
                got = jnp.where(even_lon, a, b) if side == 0 else jnp.where(even_lon, b, a)
                by = 8 if side == 0 else 4
                one, two, u, w = [
                    jnp.where(outer, roll(got, by - 4 * slot), own_ref[slot, rows, :]) for slot in range(4)
                ]
                m_ref[side, 0, at, :] = one
                m_ref[side, 1, at, :] = two
                s_ref[side, B, at, :] = over_groups(first * one + second * two)
                f_ref[side, 0, at, :] = u
                f_ref[side, 1, at, :] = w
                got = over_groups(jnp.where(lane < 8, roll(surfaces[side], -8 * r), 0.0))
                s_ref[side, DEP, at, :] = jnp.where(outer, roll(got, by), own_ref[PDEP, rows, :])
                s_ref[side, DIA, at, :] = jnp.where(outer, roll(got, by - 4), own_ref[PDIA, rows, :]) - shift

        for r in range(CHUNKS):
            assemble(r)

        def images(r, carry):
            for side in range(2):
                value = shifted(s_ref.at[side, B], s_ref.at[side, DIA], r)
                s_ref[side, H, rows_at(r), :] = on_grid(r, last, value)
            return carry

        lax.fori_loop(0, CHUNKS, images, 0, unroll=10)

        def advect(r, carry):
            at, out_at = rows_at(r), aligned(8 * r)
            for side in range(2):
                mins = depths(s_ref.at[side, DEP], r)
                coef = coefficients(f_ref[side, 0, at, :], f_ref[side, 1, at, :], mins, level_of)
                one = apply(coef, *star(m_ref.at[side, 0], r))
                two = apply(coef, *star(m_ref.at[side, 1], r))
                p = apply(coef, *star(s_ref.at[side, B], r))
                q = apply(coef, *star(s_ref.at[side, H], r))
                for slot, value in enumerate((one, two, p, q)):
                    z_ref[side, slot, out_at, :] = value
                s_ref[side, U, at, :] = over_groups(first * one + second * two)
                s_ref[side, V, at, :] = over_groups(square * p)
                s_ref[side, W, at, :] = over_groups(square * q)
            return carry

        lax.fori_loop(0, CHUNKS, advect, 0, unroll=5)

        def images_two(r, carry):
            for side in range(2):
                for source, target in ((U, HU), (V, HV), (W, HW)):
                    value = shifted(s_ref.at[side, source], s_ref.at[side, DIA], r)
                    s_ref[side, target, rows_at(r), :] = on_grid(r, last, value)
            return carry

        lax.fori_loop(0, CHUNKS, images_two, 0, unroll=10)

        east = lane < 8

        def gather(r, sums):
            at = rows_at(r)

            def both(field):
                return jnp.where(east, s_ref[0, field, at, :], s_ref[1, field, at, :])

            def image(field):
                one, two = [shifted(s_ref.at[side, field], s_ref.at[side, DIA], r) for side in range(2)]
                return jnp.where(east, one, two)

            hh, *second_image = [image(field) for field in (H, HU, HV, HW)]
            b, h, *rest = [both(field) for field in (B, H, U, V, W, HU, HV, HW)]
            return tuple(s + n for s, n in zip(sums, products(b, h, hh, rest[:3], rest[3:], second_image)))

        zero = jnp.zeros((8, LANES), jnp.float32)
        sums = lax.fori_loop(1, CHUNKS - 1, gather, (zero,) * NSUMS, unroll=8)
        keep = (lane >= 4) & (lane < 12)
        for index, value in enumerate(sums):
            at = pl.ds(8 * index, 8)
            all_ref[at, :] = block_sums_ref[at, :] + jnp.where(keep, value, 0.0)
        for index in range(NSUMS, SUM_ROWS):
            all_ref[pl.ds(8 * index, 8), :] = zero
        row = lax.broadcasted_iota(jnp.int32, (8, LANES), 0)
        line = jnp.zeros((8, LANES), jnp.float32)
        for base in range(0, SUM_ROWS, 8):
            total = all_ref[pl.ds(8 * base, 8, stride=8), :]
            for sub in range(1, 8):
                total = total + all_ref[pl.ds(8 * base + sub, 8, stride=8), :]
            total = jnp.sum(total, axis=1, keepdims=True)
            line = jnp.where(lane == base + row, total, line)
        line = jnp.sum(line, axis=0, keepdims=True)
        line = jnp.where(lane[0:1, :] == NSUMS, shift[0:1, :], line)
        sums_ref[...] = jnp.broadcast_to(line, (devices, LANES))

    return kernel


def solve(m0, m1, m2, m3, m4, shift):
    def over_devices(x):
        return jnp.sum(x, axis=1, keepdims=True)

    norm = over_devices(m0)
    mean = over_devices(m1 + shift * m0) / norm
    theta = mean + SHIFT
    delta = shift - mean
    spread = over_devices(m2 + delta * (2.0 * m1 + delta * m0))
    curve = over_devices(m3 + delta * (2.0 * m2 + m4 + delta * (3.0 * m1 + delta * m0)))
    ratio = spread / (theta * theta * norm)
    gamma = curve / spread + theta * (1.0 - ratio)
    image = -1.0 / (theta * gamma)
    return 1.0 / theta + ratio / gamma + delta * image, image


def make_finish_kernel(lat_count):
    def kernel(
        c_ref, zon_ref, mer_ref, am_ref, pq_ref, s_ref, late_ref, z_ref, side_ref, sums_ref,
        out_ref, sens_ref, m_ref, zm_ref, zx_ref,
    ):
        lane = lane_iota()
        pos = lane % 16
        level_of = (lane // 16).astype(jnp.float32)
        coup = [c_ref[level] for level in range(16)]
        first, second = c_ref[16], c_ref[17]

        devices = sums_ref.shape[0]
        blocks = []
        for base in range(0, devices, LANES):
            part = sums_ref[base : min(base + LANES, devices), :]
            if part.shape[0] < LANES:
                part = jnp.concatenate([part, jnp.zeros((LANES - part.shape[0], LANES), jnp.float32)], axis=0)
            blocks.append(jnp.transpose(part))
        turned = blocks[0] if len(blocks) == 1 else jnp.concatenate(blocks, axis=1)
        rows = [turned[i : i + 1, :] for i in range(NSUMS + 1)]
        shift = rows[NSUMS]
        near, e1 = solve(*rows[:5], shift)
        factor = (None, near, e1, near * near, near * e1, e1 * e1)
        moments = []
        for kind in range(5):
            base = 5 + kind * len(PAIRS)
            value = rows[base]
            for index in range(1, len(PAIRS)):
                twice = 2.0 if kind in (0, 2) and index in (1, 2, 4) else 1.0
                value = value + (twice * factor[index]) * rows[base + index]
            moments.append(value)
        late, e0 = solve(*moments, shift)
        me = lax.axis_index("lon") * lat_count + lax.axis_index("lat")
        mine = lax.broadcasted_iota(jnp.int32, shift.shape, 1) == me
        a1, a0 = [jnp.sum(jnp.where(mine, v, 0.0), axis=1, keepdims=True) for v in (near, late)]
        a1, e1, a0, e0 = [jnp.broadcast_to(v, (8, LANES)) for v in (a1, e1, a0, e0)]

        def surface(ref, at):
            b = ref[U, at, :] + a1 * ref[V, at, :] + e1 * ref[W, at, :]
            h = ref[HU, at, :] + a1 * ref[HV, at, :] + e1 * ref[HW, at, :]
            x = a0 * b + e0 * h
            return x, x + (a1 * ref[B, at, :] + e1 * ref[H, at, :])

        def middle(r, carry):
            at, to = aligned(8 * r), rows_at(r)
            for side in range(2):
                x, both_steps = surface(side_ref.at[side], to)
                zx_ref[side, at, :] = both_steps
                part = a1 * z_ref[side, 2, at, :] + e1 * z_ref[side, 3, at, :]
                part = part + jnp.where(side_ref[side, DEP, to, :] > level_of, x, 0.0)
                zm_ref[side, 0, to, :] = z_ref[side, 0, at, :] + first * part
                zm_ref[side, 1, to, :] = z_ref[side, 1, at, :] + second * part
            x, both_steps = surface(s_ref, to)
            zx_ref[2, at, :] = both_steps
            dep = s_ref[DEP, to, :]
            for k in range(8):
                part = a1 * pq_ref[k, at, :] + e1 * pq_ref[8 + k, at, :] + jnp.where(dep > float(k), x, 0.0)
                for level in (k, k + 8):
                    m_ref[level, to, :] = am_ref[level, at, :] + coup[level] * part
            return carry

        lax.fori_loop(0, CHUNKS, middle, 0, unroll=2)

        edge = (lane < FIRST) | (lane > LAST)

        def advect(i, carry):
            r = i + 1
            out_at = aligned(8 * i)
            ext_at = aligned(8 * r)
            at, below, above = rows_at(r), rows_at(r, -1), rows_at(r, 1)
            sides = []
            for side in range(2):
                mins = depths(side_ref.at[side, DEP], r)
                coef = coefficients(late_ref[0, out_at, :], late_ref[1, out_at, :], mins, level_of)
                sides.append([apply(coef, *star(zm_ref.at[side, t], r)) for t in range(2)])
            inserts = [jnp.where(pos < 8, sides[0][t], sides[1][t]) for t in range(2)]
            ins = jnp.where(pos < 8, zx_ref[0, ext_at, :], zx_ref[1, ext_at, :])
            sens_ref[out_at, :] = jnp.where(edge, roll(ins, -8), zx_ref[2, ext_at, :])
            mins = depths(s_ref.at[DEP], r)
            for k in range(8):
                u = 0.5 * zon_ref[0, k, out_at, :].astype(jnp.float32)
                w = 0.5 * mer_ref[0, k, out_at, :].astype(jnp.float32)
                coef = coefficients(u, w, mins, float(k))
                for level in (k, k + 8):
                    centre = m_ref[level, at, :]
                    value = apply(
                        coef, centre, roll(centre, 1), roll(centre, -1),
                        m_ref[level, below, :], m_ref[level, above, :],
                    )
                    value = jnp.where(edge, roll(inserts[level // 8], -own_shift(k)), value)
                    out_ref[level, out_at, :] = value
            return carry

        lax.fori_loop(0, ROWS // 8, advect, 0, unroll=2)

    return kernel


VMEM = pl.BlockSpec(memory_space=pltpu.VMEM)
HBM = pl.BlockSpec(memory_space=pltpu.HBM)


def on_device_of(lon, lat):
    devices = lon * lat
    f32 = jnp.float32

    def array(*shape):
        return jax.ShapeDtypeStruct(shape, f32)

    smem = pl.BlockSpec(memory_space=pltpu.SMEM)
    params = pltpu.CompilerParams(vmem_limit_bytes=48 * 2**20)
    pairs = {}
    for axis, count in (("lon", lon), ("lat", lat)):
        first = [(i, i ^ 1) for i in range(count)]
        second = [(i, (i - 1) % count if i % 2 == 0 else (i + 1) % count) for i in range(count)]
        pairs[axis] = (first, second)

    def swap(axis, a, b):
        first, second = pairs[axis]
        return lax.ppermute(a, axis, first), lax.ppermute(b, axis, second)

    def on_device(adj_tracer, zonal_flow, meridional_flow, depth, coupling, surface_diag):
        adj = adj_tracer.reshape(16, ROWS, LANES)
        block_args = (adj, zonal_flow, meridional_flow, depth, surface_diag)
        msg_a, msg_b = pl.pallas_call(
            row_message_kernel,
            in_specs=[HBM] * 5,
            out_specs=[VMEM] * 2,
            out_shape=[array(MSG_ROWS, LANES)] * 2,
            scratch_shapes=[
                pltpu.VMEM((2, 16, 8, LANES), f32),
                pltpu.VMEM((2, 2, 8, 8, LANES), jnp.bfloat16),
                pltpu.VMEM((2, 8, LANES), jnp.int32),
                pltpu.VMEM((2, 8, LANES), f32),
                pltpu.SemaphoreType.DMA((10,)),
            ],
            compiler_params=pltpu.CompilerParams(vmem_limit_bytes=16*2**20),
            name="row_messages",
        )(*[pltpu.with_memory_space_constraint(x, pltpu.HBM) for x in block_args])
        recv_a, recv_b = swap("lat", msg_a, msg_b)
        shapes = [
            (SIDE_ROWS, LANES), (SIDE_ROWS, LANES), (6, EXT, LANES), (2, ROWS, LANES),
            (16, PAD, LANES), (16, PAD, LANES), (10, PAD, LANES), (18, 8, LANES),
        ]
        cols_a, cols_b, own, late, masked, flows, surface, factors = pl.pallas_call(
            pack_interior_kernel,
            in_specs=[smem] + [VMEM] * 5,
            out_specs=[VMEM] * len(shapes),
            out_shape=[array(*shape) for shape in shapes],
            compiler_params=params,
            cost_estimate=pl.CostEstimate(flops=4_000_000, bytes_accessed=1_000_000, transcendentals=0),
            name="pack_interior",
        )(coupling, *block_args)
        row_scratch = [pltpu.VMEM((MSG_ROWS, LANES), f32)] * 2
        cols_a, cols_b, own = pl.pallas_call(
            make_pack_edges_kernel(lat - 1),
            in_specs=[VMEM] * 5,
            out_specs=[VMEM] * 3,
            out_shape=[array(*shape) for shape in shapes[:3]],
            scratch_shapes=row_scratch,
            input_output_aliases={2: 0, 3: 1, 4: 2},
            compiler_params=params,
            name="pack_edges",
        )(recv_a, recv_b, cols_a, cols_b, own)
        side_a, side_b = swap("lon", cols_a, cols_b)
        am, pq, block_sums, shift, _, _, block = pl.pallas_call(
            make_block_kernel(lat - 1),
            in_specs=[VMEM] * 6,
            out_specs=[VMEM] * 7,
            out_shape=[
                array(16, EXT, LANES), array(16, EXT, LANES), array(8 * NSUMS, LANES), array(8, LANES),
                array(16, PAD, LANES), array(16, PAD, LANES), array(10, PAD, LANES),
            ],
            scratch_shapes=row_scratch,
            input_output_aliases={3: 4, 4: 5, 5: 6},
            compiler_params=params,
            cost_estimate=pl.CostEstimate(flops=16_000_000, bytes_accessed=4_000_000, transcendentals=0),
            name="block",
        )(factors, recv_a, recv_b, masked, flows, surface)
        z, sides, sums = pl.pallas_call(
            make_sides_kernel(lat - 1, devices),
            in_specs=[VMEM] * 6,
            out_specs=[VMEM] * 3,
            out_shape=[array(2, 4, EXT, LANES), array(2, 10, PAD, LANES), array(devices, LANES)],
            scratch_shapes=[
                pltpu.VMEM((2, 2, PAD, LANES), f32),
                pltpu.VMEM((2, 2, PAD, LANES), f32),
                pltpu.VMEM((8 * SUM_ROWS, LANES), f32),
            ],
            compiler_params=params,
            name="sides",
        )(factors, own, side_b, side_a, block_sums, shift)
        everyone = lax.all_to_all(sums, ("lon", "lat"), 0, 0, tiled=True)
        out, sens = pl.pallas_call(
            make_finish_kernel(lat),
            in_specs=[VMEM] * 10,
            out_specs=[VMEM] * 2,
            out_shape=[array(16, ROWS, LANES), array(ROWS, LANES)],
            scratch_shapes=[
                pltpu.VMEM((16, PAD, LANES), f32),
                pltpu.VMEM((2, 2, PAD, LANES), f32),
                pltpu.VMEM((3, EXT, LANES), f32),
            ],
            compiler_params=params,
            name="finish",
        )(factors, zonal_flow, meridional_flow, am, pq, block, late, z, sides, everyone)
        return out.reshape(adj_tracer.shape), sens

    return on_device


def solution(mesh):
    in_specs = (
        P(None, None, "lat", "lon"),
        P(None, None, "lat", "lon"),
        P(None, None, "lat", "lon"),
        P("lat", "lon"),
        P(),
        P("lat", "lon"),
    )
    out_specs = (P(None, None, "lat", "lon"), P("lat", "lon"))
    return jax.shard_map(
        on_device_of(mesh.shape["lon"], mesh.shape["lat"]),
        mesh=mesh, in_specs=in_specs, out_specs=out_specs, check_vma=False,
    )
```
